512 devices in a mesh: segment: 16 (over z), fsdp: 32 (over x, y, core).
Axes of the slice: x: 4, y: 4, z: 16, core: 2. Of those that a mesh axis runs over, the one named last changes fastest.
Arguments:
- activations: bfloat16 [16, 4096, 4096], P('segment', 'fsdp'), may hold values from -6 to 6
- output_grad: bfloat16 [16, 4096, 4096], P('segment', 'fsdp'), may hold values from -0.75 to 0.75
- blocks: bfloat16 [16, 96, 128, 128], P('segment', 'fsdp'), may hold values from -0.5 to 0.5
- block_ids: int32 [16, 96], P('segment', 'fsdp'), may hold values from 0 to 21503, as said below
- owner_counts: int32 [16, 32], P('segment', 'fsdp'), may hold values from 1 to 3, 60 in all within a row
Outputs:
- arriving: bfloat16 [16, 4096, 4096], P('segment', 'fsdp')
- block_grads: float32 [16, 96, 128, 128], P('segment', 'fsdp')
The draws below stay inside these ranges and needn't reach their ends.
Inputs may be any that keep to these rules, and one draw needn't show every extreme that they name: `block_ids`: with ND = 32 and NF = 224, an id e names kind e // (NF ND), hidden block (e // ND) mod NF and width block e mod ND. The 96 ids of one layer, padding included, name exactly 32 distinct hidden blocks, and no hidden block is named by two ids of the same kind. An owner's live blocks are its first owner_counts slots; the counts of one layer sum to exactly 60.
All inputs are finite; a program needn't handle non-finite values.
Results may differ from the reference program's by a relative error of at most 0.018.
Values may be sent and summed in bfloat16 or wider, within the bound.
A program may use at most 128 MiB of HBM per device.

```python
import math
import jax
import jax.numpy as jnp
import numpy as np
from jax import lax

D = 4096
FF = 28672
BLK = 128
HK = 112
CAP = 3
TOK_DEV = 128
SEGMENTS = 16
TOKENS = 4096
SLOTS = 96
LIVE = 60
N_FSDP = 32


def draw_block_ids(key, part):
    width_blocks = D // BLK
    hidden_blocks = FF // BLK

    def one_layer_ids(layer_key):
        first_key, second_key, third_key = jax.random.split(layer_key, 3)
        hidden_set = jax.random.permutation(first_key, hidden_blocks)[:HK]
        slot_order = jax.random.permutation(second_key, SLOTS)
        which_hidden = slot_order // 3
        slot_kind = slot_order % 3
        column = jax.random.randint(third_key, (SLOTS,), 0, width_blocks)
        return (slot_kind * hidden_blocks * width_blocks + hidden_set[which_hidden] * width_blocks + column).astype(jnp.int32)
    layer_keys = jax.random.split(key, SEGMENTS)
    return jax.vmap(one_layer_ids)(layer_keys)


def shard_levels(stream_key, shape, pieces, least, high):
    level, own = 1.0, jax.random.fold_in(stream_key, 6)
    for dim, shards_of in pieces:
        draws = jnp.exp(jax.random.uniform(jax.random.fold_in(own, dim), (shards_of,), jnp.float32, least / len(pieces), high / len(pieces)))
        level = level * jnp.repeat(draws, shape[dim] // shards_of).reshape([-1 if axis == dim else 1 for axis in range(len(shape))])
    return level


def profile(count, total, bound, skew):
    weights = [(1 << 20) // math.isqrt(rank ** skew) + 1 for rank in range(2, count + 1)]
    spare, holding = total - bound - (count - 1), [1] * (count - 1)
    while spare > 0:
        movable = [i for i in range(count - 1) if holding[i] < bound]
        whole, budget = sum([weights[i] for i in movable]), spare
        for i in movable:
            extra = min(bound - holding[i], max(1, budget * weights[i] // whole), spare)
            holding[i] = holding[i] + extra
            spare = spare - extra
    return np.array([bound] + holding)


def uneven_parts(rng, amount, total, bound, slope):
    if amount == 2:
        one = jax.random.randint(rng, (), max(1, total - bound), min(bound, total - 1) + 1)
        return jnp.stack([one, total - one])
    lengths = jnp.asarray(profile(amount, total, bound, slope), jnp.int32)
    twos = (amount - 1) // 2
    source_of, receiver = lengths[1:1 + 2 * twos:2], lengths[2:2 + 2 * twos:2]
    slack = jnp.minimum(source_of - 1, bound - receiver)
    moved = jax.random.randint(jax.random.fold_in(rng, 1), (twos,), 0, 1 << 20) % (slack + 1)
    lengths = lengths.at[1:1 + 2 * twos:2].set(source_of - moved).at[2:2 + 2 * twos:2].set(receiver + moved)
    return lengths[jax.random.permutation(jax.random.fold_in(rng, 2), amount)]


def gaussian(key, dims, scale, bound, cuts=(), kind=jnp.bfloat16):
    values = jax.random.normal(key, dims, jnp.float32) * scale
    if len(cuts) > 0:
        values = shard_levels(key, dims, cuts, -0.22, 0.18) * values
    return jnp.clip(values, min=-bound, max=bound).astype(kind)


def setup_inputs(seed: int = 0) -> dict:
    key_of = jax.random.split(jax.random.key(seed), 6)
    activations = gaussian(key_of[0], (SEGMENTS, TOKENS, D), 1.0, 6.0, ((0, 16), (1, 32)))
    output_grad = gaussian(key_of[1], (SEGMENTS, TOKENS, D), 0.125, 0.75, ((0, 16), (1, 32)))
    blocks = gaussian(key_of[2], (SEGMENTS, SLOTS, BLK, BLK), (max(BLK, LIVE * BLK // (3 * HK))) ** -0.5, 0.5, ((0, 16), (1, 32)))
    block_ids = draw_block_ids(jax.random.fold_in(key_of[5], 71), 0)
    owner_counts = jax.vmap(lambda own: uneven_parts(own, N_FSDP, LIVE, CAP, 2))(jax.random.split(key_of[4], SEGMENTS)).reshape((SEGMENTS, N_FSDP)).astype(jnp.int32)
    return {"activations": activations, "output_grad": output_grad, "blocks": blocks, "block_ids": block_ids, "owner_counts": owner_counts}


def slot_layout(block_list, count_list, slot_cap):
    width_blocks = D // BLK
    hidden_blocks = FF // BLK
    slot_kind = block_list // (hidden_blocks * width_blocks)
    hidden_index = (block_list // width_blocks) % hidden_blocks
    column = block_list % width_blocks
    position = jnp.arange(block_list.shape[0], dtype=jnp.int32)
    is_live = (position % slot_cap) < jnp.repeat(count_list, slot_cap)
    hidden_table = (hidden_index[:, None] == jnp.arange(hidden_blocks, dtype=jnp.int32)[None, :]).astype(jnp.int32)
    hidden_used = jnp.max(hidden_table, axis=0)
    hidden_rank = jnp.cumsum(hidden_used, dtype=jnp.int32) - 1
    compact = jnp.sum(hidden_table * hidden_rank[None, :], axis=1).astype(jnp.int32)
    return slot_kind, column, compact, is_live


def slot_masks(slot_kind, column, compact, is_live):
    live_float = is_live.astype(jnp.float32)
    to_hidden = (compact[:, None] == jnp.arange(HK, dtype=jnp.int32)[None, :]).astype(jnp.float32)
    to_width = (column[:, None] == jnp.arange(D // BLK, dtype=jnp.int32)[None, :]).astype(jnp.float32)
    gate_sel = to_hidden * (live_float * (slot_kind == 0))[:, None]
    up_sel = to_hidden * (live_float * (slot_kind == 1))[:, None]
    down_sel = to_hidden * (live_float * (slot_kind == 2))[:, None]
    width_sel = to_width * (live_float * (slot_kind < 2))[:, None]
    return gate_sel, up_sel, down_sel, width_sel


def settle(values):
    return lax.optimization_barrier(values.astype(jnp.bfloat16)).astype(jnp.float32)


def one_layer(layer_items):
    layer_acts, layer_grads, layer_blocks, block_list, count_list = layer_items
    slot_kind, column, compact, is_live = slot_layout(block_list, count_list, CAP)
    gate_sel, up_sel, down_sel, width_sel = slot_masks(slot_kind, column, compact, is_live)
    live_float = is_live.astype(jnp.float32)
    weights = layer_blocks.astype(jnp.float32)
    highest = lax.Precision.HIGHEST
    is_up = (slot_kind == 1)[None, :, None]
    is_down = (slot_kind == 2)[None, :, None]

    def group(grad_total, group_pair):
        token_rows, grad_rows = group_pair
        token_grid = token_rows.astype(jnp.float32).reshape(TOK_DEV, D // BLK, BLK)
        grad_grid = grad_rows.astype(jnp.float32).reshape(TOK_DEV, D // BLK, BLK)
        token_pick = jnp.take(token_grid, column, axis=1)
        product = jnp.einsum("rnc,ncd->rnd", token_pick, weights, precision=highest)
        gate_sum = jnp.einsum("rnd,nh->rhd", product, gate_sel, precision=highest)
        up_sum = jnp.einsum("rnd,nh->rhd", product, up_sel, precision=highest)
        gate_sigmoid = jax.nn.sigmoid(gate_sum)
        gate_silu = gate_sum * gate_sigmoid
        hidden = settle(gate_silu * up_sum)
        grad_pick = jnp.take(grad_grid, column, axis=1)
        back_hidden = jnp.einsum("rnd,ncd->rnc", grad_pick, weights, precision=highest)
        hidden_grad = jnp.einsum("rnc,nh->rhc", back_hidden, down_sel, precision=highest)
        gate_grad = settle(hidden_grad * up_sum * gate_sigmoid * (1.0 + gate_sum * (1.0 - gate_sigmoid)))
        up_grad = settle(hidden_grad * gate_silu)
        out_pick = jnp.where(is_up, jnp.take(up_grad, compact, axis=1), jnp.take(gate_grad, compact, axis=1))
        back_input = jnp.einsum("rnd,ncd->rnc", out_pick, weights, precision=highest)
        width_grad = jnp.einsum("rnc,ni->ric", back_input, width_sel, precision=highest)
        passed = (grad_rows.astype(jnp.float32) + width_grad.reshape(TOK_DEV, D)).astype(jnp.bfloat16)
        left_side = jnp.where(is_down, jnp.take(hidden, compact, axis=1), token_pick)
        right_side = jnp.where(is_down, grad_pick, out_pick)
        terms = jnp.einsum("rnc,rnd->ncd", left_side, right_side, precision=highest) * live_float[:, None, None]
        return grad_total + settle(terms), passed

    start_total = jnp.zeros((SLOTS, BLK, BLK), jnp.float32)
    acts_groups = layer_acts.reshape(N_FSDP, TOK_DEV, D)
    grads_groups = layer_grads.reshape(N_FSDP, TOK_DEV, D)
    grad_total, passed = lax.scan(group, start_total, (acts_groups, grads_groups))
    return passed.reshape(TOKENS, D), grad_total


def reference(activations, output_grad, blocks, block_ids, owner_counts):
    passed, totals = lax.map(one_layer, (activations, output_grad, blocks, block_ids, owner_counts))
    arriving = jnp.concatenate([passed[1:], jnp.zeros_like(passed[:1])], axis=0)
    return arriving, totals
```

```python
import jax
import jax.numpy as jnp
from jax import lax
from jax.experimental import pallas as pl
from jax.experimental.pallas import tpu as pltpu
from jax.sharding import PartitionSpec as P

D = 4096
FF = 28672
BLK = 128
CAP = 3
ND = D // BLK
NF = FF // BLK
OWNERS = 32
SLOTS = OWNERS * CAP
PIECE = CAP * BLK
GRAIN = BLK // 2
PART = PIECE // GRAIN
HALF = PART // 2
TOK = 128
TRIPLES = 20
ENTRIES = 2 * TRIPLES
ZSENDS = 8
MESH = pl.DeviceIdType.MESH

ROW_SG, ROW_SU, ROW_SD, ROW_CG, ROW_CU, ROW_CD = range(6)
ROW_TERM, ROW_OUT, ROW_WGT, ROW_SUM = range(6, 10)


def write_tables(tile, table, keep):
    shape = (128, 128)
    lane = lax.broadcasted_iota(jnp.int32, shape, 1)
    sub = lax.broadcasted_iota(jnp.int32, shape, 0)

    def across(row):
        return jnp.broadcast_to(row, shape)

    def down(row):
        return across(row).T

    def total(mask, values):
        return jnp.sum(jnp.where(mask, values, 0), axis=0, keepdims=True)

    def put(row, values):
        table[row : row + 1, :] = values

    kind, hidden, width, live = (tile[r : r + 1, :] for r in range(4))
    valid = lane[0:1] < SLOTS
    hidden = jnp.where(valid, hidden, 1000)
    thrice = total(down(hidden) < across(hidden), 1)
    key = down(jnp.where(valid, kind * SLOTS + thrice, -1))
    width_down, live_down = down(width), down(live)
    slots, widths, full = [], [], None
    for k in range(3):
        match = (key == k * SLOTS + 3 * lane) & (lane < ND)
        slots.append(down(total(match, sub)))
        widths.append(down(total(match, width_down)))
        alive = total(match, live_down)
        full = alive if full is None else full * alive
    full = down(full)
    place = down(total(sub < lane, full))
    whole = full == 1
    pick = whole & (place == lane)
    for k in range(3):
        put(ROW_SG + k, 2 * (SLOTS + total(pick, slots[k] - SLOTS)))
        put(ROW_CG + k, total(pick, widths[k]))
    hit = whole & (3 * sub == across(thrice)) & (sub < ND)
    none = 3 * TRIPLES
    put(ROW_TERM, 2 * (none + total(hit, 3 * place + across(kind) - none)))
    late = whole & (place + TRIPLES == lane)
    entry_width = 64 + total(pick, widths[0] - 64) + total(late, widths[1] - 64)
    entry_slot = SLOTS + total(pick, slots[0] - SLOTS) + total(late, slots[1] - SLOTS)
    order = entry_width * 128 + lane[0:1]
    rank = down(total(down(order) < across(order), 1))
    entry_width = down(entry_width)
    chosen = rank == lane
    put(ROW_OUT, total(chosen, sub))
    put(ROW_WGT, 2 * total(chosen, down(entry_slot)))
    same = total(chosen, entry_width) == total(rank + 1 == lane, entry_width)
    same = down(jnp.where(same & (lane[0:1] > 0), 1, 0)).astype(jnp.float32)
    for m in range(ENTRIES):
        keep[m] = jnp.broadcast_to(same[m : m + 1, :], (8, 128))
    present = total(entry_width == lane, 1) > 0
    put(ROW_SUM, jnp.where(present, total(entry_width <= lane, 1), 0))


def kernel(
    ids,
    count,
    x_hbm,
    y_hbm,
    blocks_hbm,
    arriving,
    grads,
    x_flat,
    y_flat,
    x,
    y,
    wgt,
    meta_a,
    meta_b,
    meta_c,
    table,
    tbl,
    keep,
    hid,
    out_grad,
    sums,
    passed,
    zeros,
    terms,
    sib_out,
    sib_in,
    pair_two,
    one_in,
    pair_side,
    side_in,
    quad,
    far_in,
    near_in,
    local_sem,
    send_sem,
    recv_sem,
):
    z, f = lax.axis_index("segment"), lax.axis_index("fsdp")
    layers = lax.axis_size("segment")
    core = lax.rem(f, 2)
    yy, xx = lax.rem(lax.div(f, 2), 4), lax.div(f, 8)
    a = xx * (1 - core) + yy * core
    b = xx * core + yy * (1 - core)

    def owner(da, db):
        return lax.rem(a + da, 4) * (8 - 6 * core) + lax.rem(b + db, 4) * (2 + 6 * core) + core

    def sib_owner(da, db):
        return lax.rem(b + da, 4) * (2 + 6 * core) + lax.rem(a + db, 4) * (8 - 6 * core) + 1 - core

    sibling = f + 1 - 2 * core
    used = [0]

    def remote(src, dst, target):
        i = used[0]
        used[0] = i + 1
        return pltpu.make_async_remote_copy(
            src_ref=src,
            dst_ref=dst,
            send_sem=send_sem.at[i],
            recv_sem=recv_sem.at[i],
            device_id=target,
            device_id_type=MESH,
        )

    own_in = pltpu.make_async_copy(
        blocks_hbm, wgt.at[pl.ds(f * PART, PART)], local_sem.at[0]
    )
    x_in = pltpu.make_async_copy(x_hbm, x_flat, local_sem.at[1])
    y_in = pltpu.make_async_copy(y_hbm, y_flat, local_sem.at[2])
    own_in.start()
    x_in.start()
    y_in.start()

    barrier = pltpu.get_barrier_semaphore()
    partners = [{"fsdp": owner(d, 0)} for d in (1, 2, 3)]
    partners += [{"fsdp": owner(0, d)} for d in (1, 2, 3)]
    partners += [{"fsdp": sibling}]
    partners += [{"segment": lax.rem(z + d, layers)} for d in (1, layers - 1)]
    for partner in partners:
        pl.semaphore_signal(barrier, inc=1, device_id=partner, device_id_type=MESH)

    lane = lax.broadcasted_iota(jnp.int32, (8, 128), 1)
    sub = lax.broadcasted_iota(jnp.int32, (8, 128), 0)
    tile = jnp.zeros((8, 128), jnp.int32)
    alive = jnp.full((8, 128), count[0, 0], jnp.int32)
    for s in range(CAP):
        slot_id = jnp.full((8, 128), ids[0, s], jnp.int32)
        kind = jnp.where(slot_id >= NF * ND, 1, 0) + jnp.where(slot_id >= 2 * NF * ND, 1, 0)
        hidden = (slot_id - kind * (NF * ND)) >> 5
        width = slot_id & (ND - 1)
        live = jnp.where(alive > s, 1, 0)
        column = jnp.where(sub == 0, kind, jnp.where(sub == 1, hidden, jnp.where(sub == 2, width, live)))
        tile = tile + jnp.where((lane == CAP * f + s) & (sub < 4), column, 0)
    meta_a[0] = tile
    wgt[2 * SLOTS :] = jnp.zeros((2, GRAIN, BLK), jnp.bfloat16)
    terms[6 * TRIPLES :] = jnp.zeros((2, GRAIN, BLK), jnp.bfloat16)
    sums[0] = jnp.zeros((BLK, BLK), jnp.float32)

    own_in.wait()
    pl.semaphore_wait(barrier, len(partners))

    def piece(da, db, half=None):
        start = owner(da, db) * PART + (HALF if half == 1 else 0)
        return wgt.at[pl.ds(start, PART if half is None else HALF)]

    def forward(da, db, half, target):
        ref = piece(da, db, half)
        copy = remote(ref, ref, {"fsdp": target})
        copy.start()
        return copy

    sends = []

    def to_sibling(da, db):
        copy = forward(da, db, None, sibling)
        to_sib.append(copy)
        sends.append(copy)

    def push(da, db, half, target):
        copy = forward(da, db, half, target)
        sends.append(copy)
        return copy

    def spread(da):
        return push(da, 0, None, owner(0, 1)), push(da, 0, None, owner(0, 3))

    to_sib = []
    meta_one = [remote(meta_a.at[0], meta_a.at[d], {"fsdp": owner(d, 0)}) for d in (1, 2, 3)]
    for copy in meta_one:
        copy.start()
    right, left = push(0, 0, None, owner(1, 0)), push(0, 0, None, owner(3, 0))
    row_own = spread(0)
    to_sibling(0, 0)
    for copy in meta_one:
        copy.wait_recv()
    meta_b[0] = meta_a[0] + meta_a[1] + meta_a[2] + meta_a[3]
    meta_two = [remote(meta_b.at[0], meta_b.at[d], {"fsdp": owner(0, d)}) for d in (1, 2, 3)]
    for copy in meta_two:
        copy.start()
    right.wait_recv()
    far_right = push(3, 0, 0, owner(1, 0))
    row_left = spread(3)
    to_sibling(3, 0)
    left.wait_recv()
    far_left = push(1, 0, 1, owner(3, 0))
    row_right = spread(1)
    to_sibling(1, 0)
    for copy in meta_two:
        copy.wait_recv()
    meta_c[0] = meta_b[0] + meta_b[1] + meta_b[2] + meta_b[3]
    meta_three = remote(meta_c.at[0], meta_c.at[1], {"fsdp": sibling})
    meta_three.start()

    halves = []

    def pass_on(row, da):
        row[0].wait_recv()
        first = push(da, 3, 0, owner(0, 1))
        to_sibling(da, 3)
        row[1].wait_recv()
        second = push(da, 1, 1, owner(0, 3))
        to_sibling(da, 1)
        halves.append((da, first, second))

    def finish():
        da, first, second = halves.pop(0)
        first.wait_recv()
        second.wait_recv()
        to_sibling(da, 2)

    pass_on(row_own, 0)
    far_right.wait_recv()
    far_left.wait_recv()
    row_far = spread(2)
    to_sibling(2, 0)
    meta_three.wait_recv()
    write_tables(meta_c[0] + meta_c[1], table, keep)
    to_scalar = pltpu.make_async_copy(table, tbl, local_sem.at[3])
    to_scalar.start()
    x_in.wait()
    y_in.wait()
    for i in range(ND):
        x[i] = x_flat[:, i * BLK : (i + 1) * BLK]
        y[i] = y_flat[:, i * BLK : (i + 1) * BLK]
    pass_on(row_left, 3)
    pass_on(row_right, 1)
    finish()
    pass_on(row_far, 2)
    finish()
    finish()
    finish()
    to_scalar.wait()
    for copy in to_sib:
        copy.wait_recv()

    def at(row, k):
        return tbl[row, k]

    def weight(i):
        return wgt[pl.ds(i, 2)].reshape(BLK, BLK)

    def dot(left_side, right_side, dims):
        return lax.dot_general(left_side, right_side, (dims, ((), ())), preferred_element_type=jnp.float32)

    def products(step, carry):
        for inner in range(4):
            k = step * 4 + inner
            gate = dot(x[at(ROW_CG, k)], weight(at(ROW_SG, k)), ((1,), (0,)))
            up = dot(x[at(ROW_CU, k)], weight(at(ROW_SU, k)), ((1,), (0,)))
            back = dot(y[at(ROW_CD, k)], weight(at(ROW_SD, k)), ((1,), (1,)))
            sigmoid = jax.nn.sigmoid(gate)
            silu = gate * sigmoid
            hid[k] = (silu * up).astype(jnp.bfloat16)
            out_grad[k] = (back * up * sigmoid * (1.0 + gate * (1.0 - sigmoid))).astype(
                jnp.bfloat16
            )
            out_grad[k + TRIPLES] = (back * silu).astype(jnp.bfloat16)
        return carry

    lax.fori_loop(0, TRIPLES // 4, products, 0)

    def widths(step, carry):
        made = []
        for inner in range(4):
            m = step * 4 + inner
            made.append(
                dot(
                    out_grad[at(ROW_OUT, m)],
                    weight(at(ROW_WGT, m)),
                    ((1,), (1,)),
                )
            )
        for inner in range(4):
            m = step * 4 + inner
            run = made[inner] + sums[m] * keep[m, 0:1, :]
            sums[m + 1] = run
        return carry

    lax.fori_loop(0, ENTRIES // 4, widths, 0)

    wide = D // ZSENDS
    z_sends = []
    for j in range(ZSENDS):
        for i in range(j * ND // ZSENDS, (j + 1) * ND // ZSENDS):
            passed[:, i * BLK : (i + 1) * BLK] = (
                y[i].astype(jnp.float32) + sums[at(ROW_SUM, i)]
            ).astype(jnp.bfloat16)
        here = pl.ds(j * wide, wide)
        copy = remote(
            passed.at[:, here], arriving.at[:, here], {"segment": lax.rem(z + layers - 1, layers)}
        )
        z_sends.append(copy)

        @pl.when(z > 0)
        def _(copy=copy):
            copy.start()

    def slot_terms(step, carry):
        for inner in range(2):
            k = step * 2 + inner
            made = (
                dot(x[at(ROW_CG, k)], out_grad[k], ((0,), (0,))),
                dot(x[at(ROW_CU, k)], out_grad[k + TRIPLES], ((0,), (0,))),
                dot(hid[k], y[at(ROW_CD, k)], ((0,), (0,))),
            )
            for n in range(3):
                terms[pl.ds(6 * k + 2 * n, 2)] = made[n].astype(jnp.bfloat16).reshape(2, GRAIN, BLK)
        return carry

    lax.fori_loop(0, TRIPLES // 2, slot_terms, 0)

    group = 4 * PART

    def term(device, g):
        return terms[at(ROW_TERM, CAP * device + lax.div(g, 2)) + lax.rem(g, 2)]

    def each(low, high, step):
        def run(t, carry):
            step(t)
            return carry

        lax.fori_loop(low, high, run, 0)

    sib_copies = {}
    for db in (2, 1, 3, 0):

        def pack(t, db=db):
            sib_out[db, t] = term(sib_owner(lax.div(t, PART), db), lax.rem(t, PART))

        each(0, group, pack)
        copy = remote(sib_out.at[db], sib_in.at[db], {"fsdp": sibling})
        copy.start()
        sends.append(copy)
        sib_copies[db] = copy

    def paired(db, t):
        own = term(owner(lax.div(t, PART), db), lax.rem(t, PART))
        return own.astype(jnp.float32) + sib_in[db, t].astype(jnp.float32)

    def reduce_to(src, dst, target):
        copy = remote(src, dst, {"fsdp": target})
        copy.start()
        sends.append(copy)
        return copy

    sib_copies[2].wait_recv()

    def pair_far(t):
        pair_two[t] = paired(2, t).astype(jnp.bfloat16)

    each(0, group, pair_far)
    middle = group // 2
    up_one = reduce_to(pair_two.at[0:middle], one_in.at[0:middle], owner(0, 1))
    down_one = reduce_to(pair_two.at[middle:], one_in.at[middle:], owner(0, 3))
    side_copies = []
    for n, (db, came) in enumerate(((1, up_one), (3, down_one))):

        def with_far(t, n=n, db=db):
            pair_side[n, t] = (paired(db, t) + one_in[t].astype(jnp.float32)).astype(jnp.bfloat16)

        def alone(t, n=n, db=db):
            pair_side[n, t] = paired(db, t).astype(jnp.bfloat16)

        sib_copies[db].wait_recv()
        each(middle * (1 - n), middle * (2 - n), alone)
        came.wait_recv()
        each(middle * n, middle * (n + 1), with_far)
        side_copies.append(reduce_to(pair_side.at[n], side_in.at[n], owner(0, db)))
    sib_copies[0].wait_recv()
    for copy in side_copies:
        copy.wait_recv()

    def ringed(da, t):
        i = PART * da + t
        value = term(owner(da, 0), t).astype(jnp.float32) + sib_in[0, i].astype(jnp.float32)
        return value + side_in[0, i].astype(jnp.float32) + side_in[1, i].astype(jnp.float32)

    def opposite(t):
        quad[2, t] = ringed(2, t).astype(jnp.bfloat16)

    each(0, PART, opposite)
    up_far = reduce_to(quad.at[2, 0:HALF], far_in.at[0:HALF], owner(1, 0))
    down_far = reduce_to(quad.at[2, HALF:], far_in.at[HALF:], owner(3, 0))
    near_copies = []
    for n, (da, came) in enumerate(((1, up_far), (3, down_far))):

        def with_opposite(t, da=da):
            quad[da, t] = (ringed(da, t) + far_in[t].astype(jnp.float32)).astype(jnp.bfloat16)

        def only(t, da=da):
            quad[da, t] = ringed(da, t).astype(jnp.bfloat16)

        each(HALF * (1 - n), HALF * (2 - n), only)
        came.wait_recv()
        each(HALF * n, HALF * (n + 1), with_opposite)
        near_copies.append(reduce_to(quad.at[da], near_in.at[n], owner(da, 0)))
    for copy in near_copies:
        copy.wait_recv()

    def final(t):
        grads[t] = ringed(0, t) + near_in[0, t].astype(jnp.float32) + near_in[1, t].astype(jnp.float32)

    each(0, PART, final)

    @pl.when(z == layers - 1)
    def _():
        zeros[...] = jnp.zeros(zeros.shape, jnp.bfloat16)
        fill = pltpu.make_async_copy(zeros, arriving, local_sem.at[4])
        fill.start()
        fill.wait()

    for copy in meta_one + meta_two + [meta_three] + sends:
        copy.wait_send()
    for copy in z_sends:

        @pl.when(z < layers - 1)
        def _(copy=copy):
            copy.wait_recv()

        @pl.when(z > 0)
        def _(copy=copy):
            copy.wait_send()


COPIES = 7 + 4 + 16 + 16 + ZSENDS + 4 + 4 + 4


def body(activations, output_grad, blocks, block_ids, owner_counts):
    bf16, f32 = jnp.bfloat16, jnp.float32
    hbm = pl.BlockSpec(memory_space=pltpu.HBM)
    free = pl.BlockSpec(memory_space=pl.ANY)
    smem = pl.BlockSpec(memory_space=pltpu.SMEM)
    vmem = pl.BlockSpec(memory_space=pltpu.VMEM)
    arriving, grads = pl.pallas_call(
        kernel,
        out_shape=(
            jax.ShapeDtypeStruct((TOK, D), bf16),
            jax.ShapeDtypeStruct((PART, GRAIN, BLK), f32),
        ),
        in_specs=[smem, smem, hbm, hbm, hbm],
        out_specs=(free, vmem),
        scratch_shapes=[
            pltpu.VMEM((TOK, D), bf16),
            pltpu.VMEM((TOK, D), bf16),
            pltpu.VMEM((ND, TOK, BLK), bf16),
            pltpu.VMEM((ND, TOK, BLK), bf16),
            pltpu.VMEM((2 * SLOTS + 2, GRAIN, BLK), bf16),
            pltpu.VMEM((4, 8, 128), jnp.int32),
            pltpu.VMEM((4, 8, 128), jnp.int32),
            pltpu.VMEM((2, 8, 128), jnp.int32),
            pltpu.VMEM((16, 128), jnp.int32),
            pltpu.SMEM((16, 128), jnp.int32),
            pltpu.VMEM((ENTRIES, 8, 128), f32),
            pltpu.VMEM((TRIPLES, TOK, BLK), bf16),
            pltpu.VMEM((ENTRIES, TOK, BLK), bf16),
            pltpu.VMEM((ENTRIES + 1, TOK, BLK), f32),
            pltpu.VMEM((TOK, D), bf16),
            pltpu.VMEM((TOK, D), bf16),
            pltpu.VMEM((6 * TRIPLES + 2, GRAIN, BLK), bf16),
            pltpu.VMEM((4, 4 * PART, GRAIN, BLK), bf16),
            pltpu.VMEM((4, 4 * PART, GRAIN, BLK), bf16),
            pltpu.VMEM((4 * PART, GRAIN, BLK), bf16),
            pltpu.VMEM((4 * PART, GRAIN, BLK), bf16),
            pltpu.VMEM((2, 4 * PART, GRAIN, BLK), bf16),
            pltpu.VMEM((2, 4 * PART, GRAIN, BLK), bf16),
            pltpu.VMEM((4, PART, GRAIN, BLK), bf16),
            pltpu.VMEM((PART, GRAIN, BLK), bf16),
            pltpu.VMEM((2, PART, GRAIN, BLK), bf16),
            pltpu.SemaphoreType.DMA((5,)),
            pltpu.SemaphoreType.DMA((COPIES,)),
            pltpu.SemaphoreType.DMA((COPIES,)),
        ],
        compiler_params=pltpu.CompilerParams(
            collective_id=0, has_side_effects=True, vmem_limit_bytes=48 * 1024 * 1024
        ),
        name="relay",
    )(
        block_ids,
        owner_counts,
        activations.reshape(TOK, D),
        output_grad.reshape(TOK, D),
        blocks.reshape(PART, GRAIN, BLK),
    )
    return arriving.reshape(1, TOK, D), grads.reshape(1, CAP, BLK, BLK)


def solution(mesh):
    placed = (
        P("segment", "fsdp", None),
        P("segment", "fsdp", None),
        P("segment", "fsdp", None, None),
        P("segment", "fsdp"),
        P("segment", "fsdp"),
    )
    return jax.shard_map(
        body,
        mesh=mesh,
        in_specs=placed,
        out_specs=(P("segment", "fsdp", None), P("segment", "fsdp", None, None)),
        check_vma=False,
    )
```

```python
import jax
import jax.numpy as jnp
from jax import lax
from jax.experimental import pallas as pl
from jax.experimental.pallas import tpu as pltpu
from jax.sharding import PartitionSpec as P

D = 4096
FF = 28672
BLK = 128
CAP = 3
ND = D // BLK
NF = FF // BLK
OWNERS = 32
SLOTS = OWNERS * CAP
PIECE = CAP * BLK
GRAIN = BLK // 2
PART = PIECE // GRAIN
HALF = PART // 2
TOK = 128
TRIPLES = 20
ENTRIES = 2 * TRIPLES
ZSENDS = 8
MESH = pl.DeviceIdType.MESH

ROW_SG, ROW_SU, ROW_SD, ROW_CG, ROW_CU, ROW_CD = range(6)
ROW_LEFT, ROW_RIGHT, ROW_OUT, ROW_WGT, ROW_SUM = range(6, 11)
AT_Y, AT_GATE, AT_UP, AT_ZERO = ND, 2 * ND, 2 * ND + TRIPLES, 2 * ND + ENTRIES
AT_HID, AT_NONE = ND, ND + TRIPLES


def write_tables(tile, table, keep):
    shape = (128, 128)
    lane = lax.broadcasted_iota(jnp.int32, shape, 1)
    sub = lax.broadcasted_iota(jnp.int32, shape, 0)

    def across(row):
        return jnp.broadcast_to(row, shape)

    def down(row):
        return across(row).T

    def total(mask, values):
        return jnp.sum(jnp.where(mask, values, 0), axis=0, keepdims=True)

    def put(row, values):
        table[row : row + 1, :] = values

    kind, hidden, width, live = (tile[r : r + 1, :] for r in range(4))
    valid = lane[0:1] < SLOTS
    hidden = jnp.where(valid, hidden, 1000)
    thrice = total(down(hidden) < across(hidden), 1)
    key = down(jnp.where(valid, kind * SLOTS + thrice, -1))
    width_down, live_down = down(width), down(live)
    slots, widths, full = [], [], None
    for k in range(3):
        match = (key == k * SLOTS + 3 * lane) & (lane < ND)
        slots.append(down(total(match, sub)))
        widths.append(down(total(match, width_down)))
        alive = total(match, live_down)
        full = alive if full is None else full * alive
    full = down(full)
    place = down(total(sub < lane, full))
    whole = full == 1
    pick = whole & (place == lane)
    for k in range(3):
        put(ROW_SG + k, 2 * (SLOTS + total(pick, slots[k] - SLOTS)))
        put(ROW_CG + k, total(pick, widths[k]) + (AT_Y if k == 2 else 0))
    hit = whole & (3 * sub == across(thrice)) & (sub < ND)
    found, spot = total(hit, 1), total(hit, place)
    left = jnp.where(kind == 2, AT_HID + spot, width)
    right = jnp.where(kind == 2, AT_Y + width, AT_GATE + TRIPLES * kind + spot)
    put(ROW_LEFT, AT_NONE + found * (left - AT_NONE))
    put(ROW_RIGHT, AT_ZERO + found * (right - AT_ZERO))
    late = whole & (place + TRIPLES == lane)
    entry_width = 64 + total(pick, widths[0] - 64) + total(late, widths[1] - 64)
    entry_slot = SLOTS + total(pick, slots[0] - SLOTS) + total(late, slots[1] - SLOTS)
    order = entry_width * 128 + lane[0:1]
    rank = down(total(down(order) < across(order), 1))
    entry_width = down(entry_width)
    chosen = rank == lane
    put(ROW_OUT, AT_GATE + total(chosen, sub))
    put(ROW_WGT, 2 * total(chosen, down(entry_slot)))
    same = total(chosen, entry_width) == total(rank + 1 == lane, entry_width)
    same = down(jnp.where(same & (lane[0:1] > 0), 1, 0)).astype(jnp.float32)
    for m in range(ENTRIES):
        keep[m] = jnp.broadcast_to(same[m : m + 1, :], (8, 128))
    present = total(entry_width == lane, 1) > 0
    put(ROW_SUM, jnp.where(present, total(entry_width <= lane, 1), 0))


def kernel(
    ids,
    count,
    x_hbm,
    y_hbm,
    blocks_hbm,
    arriving,
    grads,
    x_flat,
    y_flat,
    plain,
    turned,
    wgt,
    meta_a,
    meta_b,
    meta_c,
    table,
    tbl,
    keep,
    sums,
    passed,
    zeros,
    sib_out,
    sib_in,
    pair_out,
    side_in,
    quad,
    near_in,
    local_sem,
    send_sem,
    recv_sem,
):
    z, f = lax.axis_index("segment"), lax.axis_index("fsdp")
    layers = lax.axis_size("segment")
    core = lax.rem(f, 2)
    yy, xx = lax.rem(lax.div(f, 2), 4), lax.div(f, 8)
    a = xx * (1 - core) + yy * core
    b = xx * core + yy * (1 - core)

    def owner(da, db):
        return lax.rem(a + da, 4) * (8 - 6 * core) + lax.rem(b + db, 4) * (2 + 6 * core) + core

    def sib_owner(da, db):
        return lax.rem(b + da, 4) * (2 + 6 * core) + lax.rem(a + db, 4) * (8 - 6 * core) + 1 - core

    sibling = f + 1 - 2 * core
    used = [0]

    def remote(src, dst, target):
        i = used[0]
        used[0] = i + 1
        return pltpu.make_async_remote_copy(
            src_ref=src,
            dst_ref=dst,
            send_sem=send_sem.at[i],
            recv_sem=recv_sem.at[i],
            device_id=target,
            device_id_type=MESH,
        )

    own_in = pltpu.make_async_copy(
        blocks_hbm, wgt.at[pl.ds(f * PART, PART)], local_sem.at[0]
    )
    x_in = pltpu.make_async_copy(x_hbm, x_flat, local_sem.at[1])
    y_in = pltpu.make_async_copy(y_hbm, y_flat, local_sem.at[2])
    own_in.start()
    x_in.start()
    y_in.start()

    barrier = pltpu.get_barrier_semaphore()
    partners = [{"fsdp": owner(d, 0)} for d in (1, 2, 3)]
    partners += [{"fsdp": owner(0, d)} for d in (1, 2, 3)]
    partners += [{"fsdp": sibling}]
    partners += [{"segment": lax.rem(z + d, layers)} for d in (1, layers - 1)]
    for partner in partners:
        pl.semaphore_signal(barrier, inc=1, device_id=partner, device_id_type=MESH)

    lane = lax.broadcasted_iota(jnp.int32, (8, 128), 1)
    sub = lax.broadcasted_iota(jnp.int32, (8, 128), 0)
    tile = jnp.zeros((8, 128), jnp.int32)
    alive = jnp.full((8, 128), count[0, 0], jnp.int32)
    for s in range(CAP):
        slot_id = jnp.full((8, 128), ids[0, s], jnp.int32)
        kind = jnp.where(slot_id >= NF * ND, 1, 0) + jnp.where(slot_id >= 2 * NF * ND, 1, 0)
        hidden = (slot_id - kind * (NF * ND)) >> 5
        width = slot_id & (ND - 1)
        live = jnp.where(alive > s, 1, 0)
        column = jnp.where(sub == 0, kind, jnp.where(sub == 1, hidden, jnp.where(sub == 2, width, live)))
        tile = tile + jnp.where((lane == CAP * f + s) & (sub < 4), column, 0)
    meta_a[0] = tile
    wgt[2 * SLOTS :] = jnp.zeros((2, GRAIN, BLK), jnp.bfloat16)
    plain[AT_ZERO] = jnp.zeros((TOK, BLK), jnp.bfloat16)
    turned[AT_NONE] = jnp.zeros((BLK, TOK), jnp.bfloat16)
    sums[0] = jnp.zeros((BLK, BLK), jnp.float32)

    own_in.wait()
    pl.semaphore_wait(barrier, len(partners))

    def piece(da, db, half=None):
        start = owner(da, db) * PART + (HALF if half == 1 else 0)
        return wgt.at[pl.ds(start, PART if half is None else HALF)]

    def forward(da, db, half, target):
        ref = piece(da, db, half)
        copy = remote(ref, ref, {"fsdp": target})
        copy.start()
        return copy

    sends = []

    def to_sibling(da, db):
        copy = forward(da, db, None, sibling)
        to_sib.append(copy)
        sends.append(copy)

    def push(da, db, half, target):
        copy = forward(da, db, half, target)
        sends.append(copy)
        return copy

    def spread(da):
        return push(da, 0, None, owner(0, 1)), push(da, 0, None, owner(0, 3))

    to_sib = []
    meta_one = [remote(meta_a.at[0], meta_a.at[d], {"fsdp": owner(d, 0)}) for d in (1, 2, 3)]
    for copy in meta_one:
        copy.start()
    right, left = push(0, 0, None, owner(1, 0)), push(0, 0, None, owner(3, 0))
    opposite = push(0, 0, None, owner(2, 0))
    row_own = spread(0)
    to_sibling(0, 0)
    for copy in meta_one:
        copy.wait_recv()
    meta_b[0] = meta_a[0] + meta_a[1] + meta_a[2] + meta_a[3]
    meta_two = [remote(meta_b.at[0], meta_b.at[d], {"fsdp": owner(0, d)}) for d in (1, 2, 3)]
    for copy in meta_two:
        copy.start()
    right.wait_recv()
    row_left = spread(3)
    to_sibling(3, 0)
    left.wait_recv()
    row_right = spread(1)
    to_sibling(1, 0)
    for copy in meta_two:
        copy.wait_recv()
    meta_c[0] = meta_b[0] + meta_b[1] + meta_b[2] + meta_b[3]
    meta_three = remote(meta_c.at[0], meta_c.at[1], {"fsdp": sibling})
    meta_three.start()

    halves = []

    def pass_on(row, da):
        row[0].wait_recv()
        first = push(da, 3, 0, owner(0, 1))
        to_sibling(da, 3)
        row[1].wait_recv()
        second = push(da, 1, 1, owner(0, 3))
        to_sibling(da, 1)
        halves.append((da, first, second))

    def finish():
        da, first, second = halves.pop(0)
        first.wait_recv()
        second.wait_recv()
        to_sibling(da, 2)

    pass_on(row_own, 0)
    opposite.wait_recv()
    row_far = spread(2)
    to_sibling(2, 0)
    meta_three.wait_recv()
    write_tables(meta_c[0] + meta_c[1], table, keep)
    to_scalar = pltpu.make_async_copy(table, tbl, local_sem.at[3])
    to_scalar.start()
    x_in.wait()
    y_in.wait()
    for i in range(ND):
        block = x_flat[:, i * BLK : (i + 1) * BLK]
        plain[i] = block
        turned[i] = block.T
        plain[AT_Y + i] = y_flat[:, i * BLK : (i + 1) * BLK]
    pass_on(row_left, 3)
    pass_on(row_right, 1)
    finish()
    pass_on(row_far, 2)
    finish()
    finish()
    finish()
    to_scalar.wait()
    for copy in to_sib:
        copy.wait_recv()

    def at(row, k):
        return tbl[row, k]

    def weight(i):
        return wgt[pl.ds(i, 2)].reshape(BLK, BLK)

    def dot(left_side, right_side, dims):
        return lax.dot_general(left_side, right_side, (dims, ((), ())), preferred_element_type=jnp.float32)

    def products(step, carry):
        for inner in range(4):
            k = step * 4 + inner
            gate = dot(plain[at(ROW_CG, k)], weight(at(ROW_SG, k)), ((1,), (0,)))
            up = dot(plain[at(ROW_CU, k)], weight(at(ROW_SU, k)), ((1,), (0,)))
            back = dot(plain[at(ROW_CD, k)], weight(at(ROW_SD, k)), ((1,), (1,)))
            sigmoid = jax.nn.sigmoid(gate)
            silu = gate * sigmoid
            turned[AT_HID + k] = (silu * up).astype(jnp.bfloat16).T
            plain[AT_GATE + k] = (back * up * sigmoid * (1.0 + gate * (1.0 - sigmoid))).astype(jnp.bfloat16)
            plain[AT_UP + k] = (back * silu).astype(jnp.bfloat16)
        return carry

    lax.fori_loop(0, TRIPLES // 4, products, 0)

    def widths(step, carry):
        made = []
        for inner in range(4):
            m = step * 4 + inner
            made.append(dot(plain[at(ROW_OUT, m)], weight(at(ROW_WGT, m)), ((1,), (1,))))
        for inner in range(4):
            m = step * 4 + inner
            run = made[inner] + sums[m] * keep[m, 0:1, :]
            sums[m + 1] = run
        return carry

    wide = D // ZSENDS
    z_sends = []
    for j in range(ZSENDS):
        here = pl.ds(j * wide, wide)
        z_sends.append(
            remote(passed.at[:, here], arriving.at[:, here], {"segment": lax.rem(z + layers - 1, layers)})
        )

    @pl.when(z > 0)
    def _():
        lax.fori_loop(0, ENTRIES // 4, widths, 0)
        for j in range(ZSENDS):
            for i in range(j * ND // ZSENDS, (j + 1) * ND // ZSENDS):
                passed[:, i * BLK : (i + 1) * BLK] = (
                    plain[AT_Y + i].astype(jnp.float32) + sums[at(ROW_SUM, i)]
                ).astype(jnp.bfloat16)
            z_sends[j].start()

    def term(device, s):
        n = CAP * device + s
        return dot(turned[at(ROW_LEFT, n)], plain[at(ROW_RIGHT, n)], ((1,), (0,)))

    def launch(src, dst, target):
        copy = remote(src, dst, {"fsdp": target})
        copy.start()
        sends.append(copy)
        return copy

    order = (2, 1, 3, 0)
    sib_copies = {}
    for da in order:

        def fill(step, carry, da=da):
            for inner in range(2):
                db = 2 * step + inner
                for s in range(CAP):
                    sib_out[da, CAP * db + s] = term(sib_owner(da, db), s).astype(jnp.bfloat16)
            return carry

        lax.fori_loop(0, 2, fill, 0)
        sib_copies[da] = launch(sib_out.at[da], sib_in.at[da], sibling)
    side_copies = {}
    for da in order:
        sib_copies[da].wait_recv()

        def pair(step, carry, da=da):
            for inner in range(2):
                db = 2 * step + inner
                for s in range(CAP):
                    i = CAP * db + s
                    value = term(owner(da, db), s) + sib_in[da, i].astype(jnp.float32)
                    pair_out[da, i] = value.astype(jnp.bfloat16)
            return carry

        lax.fori_loop(0, 2, pair, 0)
        side_copies[da] = [
            launch(pair_out.at[da, pl.ds(CAP * db, CAP)], side_in.at[da, pl.ds(CAP * (db - 1), CAP)], owner(0, db))
            for db in (2, 1, 3)
        ]

    def ringed(da, s):
        value = pair_out[da, s].astype(jnp.float32)
        for n in range(3):
            value = value + side_in[da, CAP * n + s].astype(jnp.float32)
        return value

    near_copies = []
    for da in order[:3]:
        for copy in side_copies[da]:
            copy.wait_recv()
        for s in range(CAP):
            quad[da - 1, s] = ringed(da, s).astype(jnp.bfloat16)
        near_copies.append(launch(quad.at[da - 1], near_in.at[da - 1], owner(da, 0)))
    for copy in side_copies[0] + near_copies:
        copy.wait_recv()
    for s in range(CAP):
        value = ringed(0, s)
        for n in range(3):
            value = value + near_in[n, s].astype(jnp.float32)
        grads[s] = value

    @pl.when(z == layers - 1)
    def _():
        zeros[...] = jnp.zeros(zeros.shape, jnp.bfloat16)
        fill = pltpu.make_async_copy(zeros, arriving, local_sem.at[4])
        fill.start()
        fill.wait()

    for copy in meta_one + meta_two + [meta_three] + sends:
        copy.wait_send()
    for copy in z_sends:

        @pl.when(z < layers - 1)
        def _(copy=copy):
            copy.wait_recv()

        @pl.when(z > 0)
        def _(copy=copy):
            copy.wait_send()


COPIES = 7 + 3 + 16 + 16 + ZSENDS + 4 + 12 + 3


def body(activations, output_grad, blocks, block_ids, owner_counts):
    bf16, f32 = jnp.bfloat16, jnp.float32
    hbm = pl.BlockSpec(memory_space=pltpu.HBM)
    free = pl.BlockSpec(memory_space=pl.ANY)
    smem = pl.BlockSpec(memory_space=pltpu.SMEM)
    vmem = pl.BlockSpec(memory_space=pltpu.VMEM)
    arriving, grads = pl.pallas_call(
        kernel,
        out_shape=(
            jax.ShapeDtypeStruct((TOK, D), bf16),
            jax.ShapeDtypeStruct((CAP, BLK, BLK), f32),
        ),
        in_specs=[smem, smem, hbm, hbm, hbm],
        out_specs=(free, vmem),
        scratch_shapes=[
            pltpu.VMEM((TOK, D), bf16),
            pltpu.VMEM((TOK, D), bf16),
            pltpu.VMEM((AT_ZERO + 1, TOK, BLK), bf16),
            pltpu.VMEM((AT_NONE + 1, BLK, TOK), bf16),
            pltpu.VMEM((2 * SLOTS + 2, GRAIN, BLK), bf16),
            pltpu.VMEM((4, 8, 128), jnp.int32),
            pltpu.VMEM((4, 8, 128), jnp.int32),
            pltpu.VMEM((2, 8, 128), jnp.int32),
            pltpu.VMEM((16, 128), jnp.int32),
            pltpu.SMEM((16, 128), jnp.int32),
            pltpu.VMEM((ENTRIES, 8, 128), f32),
            pltpu.VMEM((ENTRIES + 1, TOK, BLK), f32),
            pltpu.VMEM((TOK, D), bf16),
            pltpu.VMEM((TOK, D), bf16),
            pltpu.VMEM((4, 4 * CAP, BLK, BLK), bf16),
            pltpu.VMEM((4, 4 * CAP, BLK, BLK), bf16),
            pltpu.VMEM((4, 4 * CAP, BLK, BLK), bf16),
            pltpu.VMEM((4, 3 * CAP, BLK, BLK), bf16),
            pltpu.VMEM((3, CAP, BLK, BLK), bf16),
            pltpu.VMEM((3, CAP, BLK, BLK), bf16),
            pltpu.SemaphoreType.DMA((5,)),
            pltpu.SemaphoreType.DMA((COPIES,)),
            pltpu.SemaphoreType.DMA((COPIES,)),
        ],
        compiler_params=pltpu.CompilerParams(
            collective_id=0, has_side_effects=True, vmem_limit_bytes=60 * 1024 * 1024
        ),
        name="relay",
    )(
        block_ids,
        owner_counts,
        activations.reshape(TOK, D),
        output_grad.reshape(TOK, D),
        blocks.reshape(PART, GRAIN, BLK),
    )
    return arriving.reshape(1, TOK, D), grads.reshape(1, CAP, BLK, BLK)


def solution(mesh):
    placed = (
        P("segment", "fsdp", None),
        P("segment", "fsdp", None),
        P("segment", "fsdp", None, None),
        P("segment", "fsdp"),
        P("segment", "fsdp"),
    )
    return jax.shard_map(
        body,
        mesh=mesh,
        in_specs=placed,
        out_specs=(P("segment", "fsdp", None), P("segment", "fsdp", None, None)),
        check_vma=False,
    )
```

```python
import jax
import jax.numpy as jnp
from jax import lax
from jax.experimental import pallas as pl
from jax.experimental.pallas import tpu as pltpu
from jax.sharding import PartitionSpec as P

D = 4096
FF = 28672
BLK = 128
CAP = 3
ND = D // BLK
NF = FF // BLK
OWNERS = 32
SLOTS = OWNERS * CAP
PIECE = CAP * BLK
GRAIN = BLK // 2
PART = PIECE // GRAIN
HALF = PART // 2
TOK = 128
TRIPLES = 20
ENTRIES = 2 * TRIPLES
CHUNK = 64
CUTS = 4
ZSENDS = CUTS * (TOK // CHUNK)
MESH = pl.DeviceIdType.MESH

ROW_SG, ROW_SU, ROW_SD, ROW_CG, ROW_CU, ROW_CD = range(6)
ROW_LEFT, ROW_RIGHT, ROW_OUT, ROW_WGT, ROW_SUM = range(6, 11)
AT_Y, AT_GATE, AT_UP, AT_ZERO = ND, 2 * ND, 2 * ND + TRIPLES, 2 * ND + ENTRIES
AT_HID, AT_NONE = ND, ND + TRIPLES


def write_tables(tile, table, keep):
    shape = (128, 128)
    lane = lax.broadcasted_iota(jnp.int32, shape, 1)
    sub = lax.broadcasted_iota(jnp.int32, shape, 0)

    def across(row):
        return jnp.broadcast_to(row, shape)

    def down(row):
        return across(row).T

    def total(mask, values):
        return jnp.sum(jnp.where(mask, values, 0), axis=0, keepdims=True)

    def put(row, values):
        table[row : row + 1, :] = values

    kind, hidden, width, live = (tile[r : r + 1, :] for r in range(4))
    valid = lane[0:1] < SLOTS
    hidden = jnp.where(valid, hidden, 1000)
    thrice = total(down(hidden) < across(hidden), 1)
    key = down(jnp.where(valid, kind * SLOTS + thrice, -1))
    width_down, live_down = down(width), down(live)
    slots, widths, full = [], [], None
    for k in range(3):
        match = (key == k * SLOTS + 3 * lane) & (lane < ND)
        slots.append(down(total(match, sub)))
        widths.append(down(total(match, width_down)))
        alive = total(match, live_down)
        full = alive if full is None else full * alive
    full = down(full)
    place = down(total(sub < lane, full))
    whole = full == 1
    pick = whole & (place == lane)
    for k in range(3):
        put(ROW_SG + k, 2 * (SLOTS + total(pick, slots[k] - SLOTS)))
        put(ROW_CG + k, total(pick, widths[k]) + (AT_Y if k == 2 else 0))
    hit = whole & (3 * sub == across(thrice)) & (sub < ND)
    found, spot = total(hit, 1), total(hit, place)
    left = jnp.where(kind == 2, AT_HID + spot, width)
    right = jnp.where(kind == 2, AT_Y + width, AT_GATE + TRIPLES * kind + spot)
    put(ROW_LEFT, AT_NONE + found * (left - AT_NONE))
    put(ROW_RIGHT, AT_ZERO + found * (right - AT_ZERO))
    late = whole & (place + TRIPLES == lane)
    entry_width = 64 + total(pick, widths[0] - 64) + total(late, widths[1] - 64)
    entry_slot = SLOTS + total(pick, slots[0] - SLOTS) + total(late, slots[1] - SLOTS)
    order = entry_width * 128 + lane[0:1]
    rank = down(total(down(order) < across(order), 1))
    entry_width = down(entry_width)
    chosen = rank == lane
    put(ROW_OUT, AT_GATE + total(chosen, sub))
    put(ROW_WGT, 2 * total(chosen, down(entry_slot)))
    same = total(chosen, entry_width) == total(rank + 1 == lane, entry_width)
    same = down(jnp.where(same & (lane[0:1] > 0), 1, 0)).astype(jnp.float32)
    for m in range(ENTRIES):
        keep[m] = jnp.broadcast_to(same[m : m + 1, :], (8, 128))
    present = total(entry_width == lane, 1) > 0
    put(ROW_SUM, jnp.where(present, total(entry_width <= lane, 1), 0))


def kernel(
    ids,
    count,
    x_hbm,
    y_hbm,
    blocks_hbm,
    arriving,
    grads,
    x_flat,
    y_flat,
    plain,
    turned,
    wgt,
    meta_a,
    meta_b,
    meta_c,
    table,
    tbl,
    keep,
    hid,
    sums,
    passed,
    zeros,
    sib_out,
    sib_in,
    pair_out,
    side_in,
    quad,
    near_in,
    local_sem,
    send_sem,
    recv_sem,
):
    z, f = lax.axis_index("segment"), lax.axis_index("fsdp")
    layers = lax.axis_size("segment")
    core = lax.rem(f, 2)
    yy, xx = lax.rem(lax.div(f, 2), 4), lax.div(f, 8)
    a = xx * (1 - core) + yy * core
    b = xx * core + yy * (1 - core)

    def owner(da, db):
        return lax.rem(a + da, 4) * (8 - 6 * core) + lax.rem(b + db, 4) * (2 + 6 * core) + core

    def sib_owner(da, db):
        return lax.rem(b + da, 4) * (2 + 6 * core) + lax.rem(a + db, 4) * (8 - 6 * core) + 1 - core

    sibling = f + 1 - 2 * core
    used = [0]

    def remote(src, dst, target):
        i = used[0]
        used[0] = i + 1
        return pltpu.make_async_remote_copy(
            src_ref=src,
            dst_ref=dst,
            send_sem=send_sem.at[i],
            recv_sem=recv_sem.at[i],
            device_id=target,
            device_id_type=MESH,
        )

    own_in = pltpu.make_async_copy(
        blocks_hbm, wgt.at[pl.ds(f * PART, PART)], local_sem.at[0]
    )
    x_in = pltpu.make_async_copy(x_hbm, x_flat, local_sem.at[1])
    y_in = pltpu.make_async_copy(y_hbm, y_flat, local_sem.at[2])
    own_in.start()
    x_in.start()
    y_in.start()

    barrier = pltpu.get_barrier_semaphore()
    partners = [{"fsdp": owner(d, 0)} for d in (1, 2, 3)]
    partners += [{"fsdp": owner(0, d)} for d in (1, 2, 3)]
    partners += [{"fsdp": sibling}]
    partners += [{"segment": lax.rem(z + d, layers)} for d in (1, layers - 1)]
    for partner in partners:
        pl.semaphore_signal(barrier, inc=1, device_id=partner, device_id_type=MESH)

    lane = lax.broadcasted_iota(jnp.int32, (8, 128), 1)
    sub = lax.broadcasted_iota(jnp.int32, (8, 128), 0)
    tile = jnp.zeros((8, 128), jnp.int32)
    alive = jnp.full((8, 128), count[0, 0], jnp.int32)
    for s in range(CAP):
        slot_id = jnp.full((8, 128), ids[0, s], jnp.int32)
        kind = jnp.where(slot_id >= NF * ND, 1, 0) + jnp.where(slot_id >= 2 * NF * ND, 1, 0)
        hidden = (slot_id - kind * (NF * ND)) >> 5
        width = slot_id & (ND - 1)
        live = jnp.where(alive > s, 1, 0)
        column = jnp.where(sub == 0, kind, jnp.where(sub == 1, hidden, jnp.where(sub == 2, width, live)))
        tile = tile + jnp.where((lane == CAP * f + s) & (sub < 4), column, 0)
    meta_a[0] = tile
    wgt[2 * SLOTS :] = jnp.zeros((2, GRAIN, BLK), jnp.bfloat16)
    plain[AT_ZERO] = jnp.zeros((TOK, BLK), jnp.bfloat16)
    turned[AT_NONE] = jnp.zeros((BLK, TOK), jnp.bfloat16)
    sums[0] = jnp.zeros((BLK, BLK), jnp.float32)

    own_in.wait()
    pl.semaphore_wait(barrier, len(partners))

    def piece(da, db, half=None):
        start = owner(da, db) * PART + (HALF if half == 1 else 0)
        return wgt.at[pl.ds(start, PART if half is None else HALF)]

    def forward(da, db, half, target):
        ref = piece(da, db, half)
        copy = remote(ref, ref, {"fsdp": target})
        copy.start()
        return copy

    sends = []

    def to_sibling(da, db):
        copy = forward(da, db, None, sibling)
        to_sib.append(copy)
        sends.append(copy)

    def push(da, db, half, target):
        copy = forward(da, db, half, target)
        sends.append(copy)
        return copy

    def spread(da):
        return push(da, 0, None, owner(0, 1)), push(da, 0, None, owner(0, 3))

    to_sib = []
    meta_one = [remote(meta_a.at[0], meta_a.at[d], {"fsdp": owner(d, 0)}) for d in (1, 2, 3)]
    for copy in meta_one:
        copy.start()
    right, left = push(0, 0, None, owner(1, 0)), push(0, 0, None, owner(3, 0))
    opposite = push(0, 0, None, owner(2, 0))
    row_own = spread(0)
    to_sibling(0, 0)
    for copy in meta_one:
        copy.wait_recv()
    meta_b[0] = meta_a[0] + meta_a[1] + meta_a[2] + meta_a[3]
    meta_two = [remote(meta_b.at[0], meta_b.at[d], {"fsdp": owner(0, d)}) for d in (1, 2, 3)]
    for copy in meta_two:
        copy.start()
    right.wait_recv()
    row_left = spread(3)
    to_sibling(3, 0)
    left.wait_recv()
    row_right = spread(1)
    to_sibling(1, 0)
    for copy in meta_two:
        copy.wait_recv()
    meta_c[0] = meta_b[0] + meta_b[1] + meta_b[2] + meta_b[3]
    meta_three = remote(meta_c.at[0], meta_c.at[1], {"fsdp": sibling})
    meta_three.start()

    halves = []

    def pass_on(row, da):
        row[0].wait_recv()
        first = push(da, 3, 0, owner(0, 1))
        to_sibling(da, 3)
        row[1].wait_recv()
        second = push(da, 1, 1, owner(0, 3))
        to_sibling(da, 1)
        halves.append((da, first, second))

    def finish():
        da, first, second = halves.pop(0)
        first.wait_recv()
        second.wait_recv()
        to_sibling(da, 2)

    pass_on(row_own, 0)
    opposite.wait_recv()
    row_far = spread(2) + (push(2, 0, None, owner(0, 2)),)
    to_sibling(2, 0)
    meta_three.wait_recv()
    write_tables(meta_c[0] + meta_c[1], table, keep)
    to_scalar = pltpu.make_async_copy(table, tbl, local_sem.at[3])
    to_scalar.start()
    x_in.wait()
    y_in.wait()
    for i in range(ND):
        block = x_flat[:, i * BLK : (i + 1) * BLK]
        plain[i] = block
        turned[i] = block.T
        plain[AT_Y + i] = y_flat[:, i * BLK : (i + 1) * BLK]
    pass_on(row_left, 3)
    pass_on(row_right, 1)
    finish()
    row_far[0].wait_recv()
    to_sibling(2, 3)
    row_far[1].wait_recv()
    to_sibling(2, 1)
    finish()
    finish()
    row_far[2].wait_recv()
    to_sibling(2, 2)
    to_scalar.wait()
    for copy in to_sib:
        copy.wait_recv()

    def at(row, k):
        return tbl[row, k]

    def weight(i):
        return wgt[pl.ds(i, 2)].reshape(BLK, BLK)

    def dot(left_side, right_side, dims):
        return lax.dot_general(left_side, right_side, (dims, ((), ())), preferred_element_type=jnp.float32)

    def products(rows):
        def step(i, carry):
            for inner in range(4):
                k = 4 * i + inner
                gate = dot(plain[at(ROW_CG, k), rows], weight(at(ROW_SG, k)), ((1,), (0,)))
                up = dot(plain[at(ROW_CU, k), rows], weight(at(ROW_SU, k)), ((1,), (0,)))
                back = dot(plain[at(ROW_CD, k), rows], weight(at(ROW_SD, k)), ((1,), (1,)))
                sigmoid = jax.nn.sigmoid(gate)
                silu = gate * sigmoid
                hid[k, rows] = (silu * up).astype(jnp.bfloat16)
                plain[AT_GATE + k, rows] = (back * up * sigmoid * (1.0 + gate * (1.0 - sigmoid))).astype(
                    jnp.bfloat16
                )
                plain[AT_UP + k, rows] = (back * silu).astype(jnp.bfloat16)
            return carry

        lax.fori_loop(0, TRIPLES // 4, step, 0)

    def widths(rows):
        def step(i, carry):
            made = []
            for inner in range(8):
                m = 8 * i + inner
                made.append(dot(plain[at(ROW_OUT, m), rows], weight(at(ROW_WGT, m)), ((1,), (1,))))
            for inner in range(8):
                m = 8 * i + inner
                sums[m + 1, rows] = made[inner] + sums[m, rows] * keep[m, 0:1, :]
            return carry

        lax.fori_loop(0, ENTRIES // 8, step, 0)

    z_sends = []
    for n in range(ZSENDS):
        here = (pl.ds(n // CUTS * CHUNK, CHUNK), pl.ds(n % CUTS * (D // CUTS), D // CUTS))
        z_sends.append(
            remote(passed.at[here], arriving.at[here], {"segment": lax.rem(z + layers - 1, layers)})
        )

    @pl.when(z > 0)
    def _():
        for n in range(ZSENDS):
            rows = pl.ds(n // CUTS * CHUNK, CHUNK)
            if n % CUTS == 0:
                products(rows)
                widths(rows)
            for i in range(n % CUTS * ND // CUTS, (n % CUTS + 1) * ND // CUTS):
                passed[rows, i * BLK : (i + 1) * BLK] = (
                    plain[AT_Y + i, rows].astype(jnp.float32) + sums[at(ROW_SUM, i), rows]
                ).astype(jnp.bfloat16)
            z_sends[n].start()

    @pl.when(z == 0)
    def _():
        products(pl.ds(0, TOK))

    def turn(i, carry):
        for inner in range(4):
            k = 4 * i + inner
            turned[AT_HID + k] = hid[k].T
        return carry

    lax.fori_loop(0, TRIPLES // 4, turn, 0)

    def term(device, s):
        n = CAP * device + s
        return dot(turned[at(ROW_LEFT, n)], plain[at(ROW_RIGHT, n)], ((1,), (0,)))

    def launch(src, dst, target):
        copy = remote(src, dst, {"fsdp": target})
        copy.start()
        sends.append(copy)
        return copy

    order = (2, 1, 3, 0)
    sib_copies, side_copies = {}, {}

    def fill(da):
        def step(i, carry):
            for inner in range(2):
                db = 2 * i + inner
                for s in range(CAP):
                    sib_out[da, CAP * db + s] = term(sib_owner(da, db), s).astype(jnp.bfloat16)
            return carry

        lax.fori_loop(0, 2, step, 0)
        sib_copies[da] = launch(sib_out.at[da], sib_in.at[da], sibling)

    def pair(da):
        def step(i, carry):
            for inner in range(2):
                db = 2 * i + inner
                for s in range(CAP):
                    n = CAP * db + s
                    value = term(owner(da, db), s) + sib_in[da, n].astype(jnp.float32)
                    pair_out[da, n] = value.astype(jnp.bfloat16)
            return carry

        sib_copies[da].wait_recv()
        lax.fori_loop(0, 2, step, 0)
        side_copies[da] = [
            launch(pair_out.at[da, pl.ds(CAP * db, CAP)], side_in.at[da, pl.ds(CAP * (db - 1), CAP)], owner(0, db))
            for db in (2, 1, 3)
        ]

    fill(2)
    fill(1)
    fill(3)
    pair(2)
    fill(0)
    pair(1)
    pair(3)
    pair(0)

    def ringed(da, s):
        value = pair_out[da, s].astype(jnp.float32)
        for n in range(3):
            value = value + side_in[da, CAP * n + s].astype(jnp.float32)
        return value

    near_copies = []
    for da in order[:3]:
        for copy in side_copies[da]:
            copy.wait_recv()
        for s in range(CAP):
            quad[da - 1, s] = ringed(da, s).astype(jnp.bfloat16)
        near_copies.append(launch(quad.at[da - 1], near_in.at[da - 1], owner(da, 0)))
    for copy in side_copies[0] + near_copies:
        copy.wait_recv()
    for s in range(CAP):
        value = ringed(0, s)
        for n in range(3):
            value = value + near_in[n, s].astype(jnp.float32)
        grads[s] = value

    @pl.when(z == layers - 1)
    def _():
        zeros[...] = jnp.zeros(zeros.shape, jnp.bfloat16)
        fill = pltpu.make_async_copy(zeros, arriving, local_sem.at[4])
        fill.start()
        fill.wait()

    for copy in meta_one + meta_two + [meta_three] + sends:
        copy.wait_send()
    for copy in z_sends:

        @pl.when(z < layers - 1)
        def _(copy=copy):
            copy.wait_recv()

        @pl.when(z > 0)
        def _(copy=copy):
            copy.wait_send()


COPIES = 7 + 3 + 16 + 16 + ZSENDS + 4 + 12 + 3


def body(activations, output_grad, blocks, block_ids, owner_counts):
    bf16, f32 = jnp.bfloat16, jnp.float32
    hbm = pl.BlockSpec(memory_space=pltpu.HBM)
    free = pl.BlockSpec(memory_space=pl.ANY)
    smem = pl.BlockSpec(memory_space=pltpu.SMEM)
    vmem = pl.BlockSpec(memory_space=pltpu.VMEM)
    arriving, grads = pl.pallas_call(
        kernel,
        out_shape=(
            jax.ShapeDtypeStruct((TOK, D), bf16),
            jax.ShapeDtypeStruct((CAP, BLK, BLK), f32),
        ),
        in_specs=[smem, smem, hbm, hbm, hbm],
        out_specs=(free, vmem),
        scratch_shapes=[
            pltpu.VMEM((TOK, D), bf16),
            pltpu.VMEM((TOK, D), bf16),
            pltpu.VMEM((AT_ZERO + 1, TOK, BLK), bf16),
            pltpu.VMEM((AT_NONE + 1, BLK, TOK), bf16),
            pltpu.VMEM((2 * SLOTS + 2, GRAIN, BLK), bf16),
            pltpu.VMEM((4, 8, 128), jnp.int32),
            pltpu.VMEM((4, 8, 128), jnp.int32),
            pltpu.VMEM((2, 8, 128), jnp.int32),
            pltpu.VMEM((16, 128), jnp.int32),
            pltpu.SMEM((16, 128), jnp.int32),
            pltpu.VMEM((ENTRIES, 8, 128), f32),
            pltpu.VMEM((TRIPLES, TOK, BLK), bf16),
            pltpu.VMEM((ENTRIES + 1, TOK, BLK), f32),
            pltpu.VMEM((TOK, D), bf16),
            pltpu.VMEM((TOK, D), bf16),
            pltpu.VMEM((4, 4 * CAP, BLK, BLK), bf16),
            pltpu.VMEM((4, 4 * CAP, BLK, BLK), bf16),
            pltpu.VMEM((4, 4 * CAP, BLK, BLK), bf16),
            pltpu.VMEM((4, 3 * CAP, BLK, BLK), bf16),
            pltpu.VMEM((3, CAP, BLK, BLK), bf16),
            pltpu.VMEM((3, CAP, BLK, BLK), bf16),
            pltpu.SemaphoreType.DMA((5,)),
            pltpu.SemaphoreType.DMA((COPIES,)),
            pltpu.SemaphoreType.DMA((COPIES,)),
        ],
        compiler_params=pltpu.CompilerParams(
            collective_id=0, has_side_effects=True, vmem_limit_bytes=60 * 1024 * 1024
        ),
        name="relay",
    )(
        block_ids,
        owner_counts,
        activations.reshape(TOK, D),
        output_grad.reshape(TOK, D),
        blocks.reshape(PART, GRAIN, BLK),
    )
    return arriving.reshape(1, TOK, D), grads.reshape(1, CAP, BLK, BLK)


def solution(mesh):
    placed = (
        P("segment", "fsdp", None),
        P("segment", "fsdp", None),
        P("segment", "fsdp", None, None),
        P("segment", "fsdp"),
        P("segment", "fsdp"),
    )
    return jax.shard_map(
        body,
        mesh=mesh,
        in_specs=placed,
        out_specs=(P("segment", "fsdp", None), P("segment", "fsdp", None, None)),
        check_vma=False,
    )
```

```python
import jax
import jax.numpy as jnp
from jax import lax
from jax.experimental import pallas as pl
from jax.experimental.pallas import tpu as pltpu
from jax.sharding import PartitionSpec as P

D = 4096
FF = 28672
BLK = 128
CAP = 3
ND = D // BLK
NF = FF // BLK
OWNERS = 32
SLOTS = OWNERS * CAP
PIECE = CAP * BLK
GRAIN = BLK // 2
PART = PIECE // GRAIN
HALF = PART // 2
TOK = 128
TRIPLES = 20
ENTRIES = 2 * TRIPLES
CHUNK = 64
CUTS = 4
ZSENDS = CUTS * (TOK // CHUNK)
MESH = pl.DeviceIdType.MESH

ROW_SG, ROW_SU, ROW_SD, ROW_CG, ROW_CU, ROW_CD = range(6)
ROW_LEFT, ROW_RIGHT, ROW_OUT, ROW_WGT, ROW_SUM = range(6, 11)
AT_Y, AT_GATE, AT_UP, AT_ZERO = ND, 2 * ND, 2 * ND + TRIPLES, 2 * ND + ENTRIES
AT_HID, AT_NONE = ND, ND + TRIPLES


def write_tables(tile, table, keep):
    shape = (128, 128)
    lane = lax.broadcasted_iota(jnp.int32, shape, 1)
    sub = lax.broadcasted_iota(jnp.int32, shape, 0)

    def across(row):
        return jnp.broadcast_to(row, shape)

    def down(row):
        return across(row).T

    def total(mask, values):
        return jnp.sum(jnp.where(mask, values, 0), axis=0, keepdims=True)

    def put(row, values):
        table[row : row + 1, :] = values

    kind, hidden, width, live = (tile[r : r + 1, :] for r in range(4))
    valid = lane[0:1] < SLOTS
    hidden = jnp.where(valid, hidden, 1000)
    thrice = total(down(hidden) < across(hidden), 1)
    key = down(jnp.where(valid, kind * SLOTS + thrice, -1))
    width_down, live_down = down(width), down(live)
    slots, widths, full = [], [], None
    for k in range(3):
        match = (key == k * SLOTS + 3 * lane) & (lane < ND)
        slots.append(down(total(match, sub)))
        widths.append(down(total(match, width_down)))
        alive = total(match, live_down)
        full = alive if full is None else full * alive
    full = down(full)
    place = down(total(sub < lane, full))
    whole = full == 1
    pick = whole & (place == lane)
    for k in range(3):
        put(ROW_SG + k, 2 * (SLOTS + total(pick, slots[k] - SLOTS)))
        put(ROW_CG + k, total(pick, widths[k]) + (AT_Y if k == 2 else 0))
    hit = whole & (3 * sub == across(thrice)) & (sub < ND)
    found, spot = total(hit, 1), total(hit, place)
    left = jnp.where(kind == 2, AT_HID + spot, width)
    right = jnp.where(kind == 2, AT_Y + width, AT_GATE + TRIPLES * kind + spot)
    put(ROW_LEFT, AT_NONE + found * (left - AT_NONE))
    put(ROW_RIGHT, AT_ZERO + found * (right - AT_ZERO))
    late = whole & (place + TRIPLES == lane)
    entry_width = 64 + total(pick, widths[0] - 64) + total(late, widths[1] - 64)
    entry_slot = SLOTS + total(pick, slots[0] - SLOTS) + total(late, slots[1] - SLOTS)
    order = entry_width * 128 + lane[0:1]
    rank = down(total(down(order) < across(order), 1))
    entry_width = down(entry_width)
    chosen = rank == lane
    put(ROW_OUT, AT_GATE + total(chosen, sub))
    put(ROW_WGT, 2 * total(chosen, down(entry_slot)))
    same = total(chosen, entry_width) == total(rank + 1 == lane, entry_width)
    same = down(jnp.where(same & (lane[0:1] > 0), 1, 0)).astype(jnp.float32)
    for m in range(ENTRIES):
        keep[m] = jnp.broadcast_to(same[m : m + 1, :], (8, 128))
    present = total(entry_width == lane, 1) > 0
    put(ROW_SUM, jnp.where(present, total(entry_width <= lane, 1), 0))


def kernel(
    ids,
    count,
    x_hbm,
    y_hbm,
    blocks_hbm,
    arriving,
    grads,
    x_flat,
    y_flat,
    plain,
    turned,
    wgt,
    meta_a,
    meta_b,
    meta_c,
    table,
    tbl,
    keep,
    hid,
    sums,
    passed,
    zeros,
    sib_out,
    sib_in,
    pair_out,
    side_in,
    quad,
    near_in,
    total,
    local_sem,
    send_sem,
    recv_sem,
):
    z, f = lax.axis_index("segment"), lax.axis_index("fsdp")
    layers = lax.axis_size("segment")
    core = lax.rem(f, 2)
    yy, xx = lax.rem(lax.div(f, 2), 4), lax.div(f, 8)
    a = xx * (1 - core) + yy * core
    b = xx * core + yy * (1 - core)

    def owner(da, db):
        return lax.rem(a + da, 4) * (8 - 6 * core) + lax.rem(b + db, 4) * (2 + 6 * core) + core

    def sib_owner(da, db):
        return lax.rem(b + da, 4) * (2 + 6 * core) + lax.rem(a + db, 4) * (8 - 6 * core) + 1 - core

    sibling = f + 1 - 2 * core
    used = [0]

    def remote(src, dst, target):
        i = used[0]
        used[0] = i + 1
        return pltpu.make_async_remote_copy(
            src_ref=src,
            dst_ref=dst,
            send_sem=send_sem.at[i],
            recv_sem=recv_sem.at[i],
            device_id=target,
            device_id_type=MESH,
        )

    own_in = pltpu.make_async_copy(
        blocks_hbm, wgt.at[pl.ds(f * PART, PART)], local_sem.at[0]
    )
    x_in = pltpu.make_async_copy(x_hbm, x_flat, local_sem.at[1])
    y_in = pltpu.make_async_copy(y_hbm, y_flat, local_sem.at[2])
    own_in.start()
    x_in.start()
    y_in.start()

    barrier = pltpu.get_barrier_semaphore()
    partners = [{"fsdp": owner(d, 0)} for d in (1, 2, 3)]
    partners += [{"fsdp": owner(0, d)} for d in (1, 2, 3)]
    partners += [{"fsdp": sibling}]
    partners += [{"segment": lax.rem(z + d, layers)} for d in (1, layers - 1)]
    for partner in partners:
        pl.semaphore_signal(barrier, inc=1, device_id=partner, device_id_type=MESH)

    lane = lax.broadcasted_iota(jnp.int32, (8, 128), 1)
    sub = lax.broadcasted_iota(jnp.int32, (8, 128), 0)
    tile = jnp.zeros((8, 128), jnp.int32)
    alive = jnp.full((8, 128), count[0, 0], jnp.int32)
    for s in range(CAP):
        slot_id = jnp.full((8, 128), ids[0, s], jnp.int32)
        kind = jnp.where(slot_id >= NF * ND, 1, 0) + jnp.where(slot_id >= 2 * NF * ND, 1, 0)
        hidden = (slot_id - kind * (NF * ND)) >> 5
        width = slot_id & (ND - 1)
        live = jnp.where(alive > s, 1, 0)
        column = jnp.where(sub == 0, kind, jnp.where(sub == 1, hidden, jnp.where(sub == 2, width, live)))
        tile = tile + jnp.where((lane == CAP * f + s) & (sub < 4), column, 0)
    meta_a[0] = tile
    wgt[2 * SLOTS :] = jnp.zeros((2, GRAIN, BLK), jnp.bfloat16)
    plain[AT_ZERO] = jnp.zeros((TOK, BLK), jnp.bfloat16)
    turned[AT_NONE] = jnp.zeros((BLK, TOK), jnp.bfloat16)
    sums[0] = jnp.zeros((BLK, BLK), jnp.float32)

    blank = pltpu.make_async_copy(zeros, arriving, local_sem.at[4])

    @pl.when(z == layers - 1)
    def _():
        zeros[...] = jnp.zeros(zeros.shape, jnp.bfloat16)
        blank.start()

    own_in.wait()
    pl.semaphore_wait(barrier, len(partners))

    def piece(da, db, half=None):
        start = owner(da, db) * PART + (HALF if half == 1 else 0)
        return wgt.at[pl.ds(start, PART if half is None else HALF)]

    def forward(da, db, half, target):
        ref = piece(da, db, half)
        copy = remote(ref, ref, {"fsdp": target})
        copy.start()
        return copy

    sends = []

    def to_sibling(da, db):
        copy = forward(da, db, None, sibling)
        to_sib.append(copy)
        sends.append(copy)

    def push(da, db, half, target):
        copy = forward(da, db, half, target)
        sends.append(copy)
        return copy

    def spread(da):
        return push(da, 0, None, owner(0, 1)), push(da, 0, None, owner(0, 3))

    to_sib = []
    meta_one = [remote(meta_a.at[0], meta_a.at[d], {"fsdp": owner(d, 0)}) for d in (1, 2, 3)]
    for copy in meta_one:
        copy.start()
    right, left = push(0, 0, None, owner(1, 0)), push(0, 0, None, owner(3, 0))
    opposite = push(0, 0, None, owner(2, 0))
    row_own = spread(0)
    to_sibling(0, 0)
    for copy in meta_one:
        copy.wait_recv()
    meta_b[0] = meta_a[0] + meta_a[1] + meta_a[2] + meta_a[3]
    meta_two = [remote(meta_b.at[0], meta_b.at[d], {"fsdp": owner(0, d)}) for d in (1, 2, 3)]
    for copy in meta_two:
        copy.start()
    right.wait_recv()
    row_left = spread(3)
    to_sibling(3, 0)
    left.wait_recv()
    row_right = spread(1)
    to_sibling(1, 0)
    for copy in meta_two:
        copy.wait_recv()
    meta_c[0] = meta_b[0] + meta_b[1] + meta_b[2] + meta_b[3]
    meta_three = remote(meta_c.at[0], meta_c.at[1], {"fsdp": sibling})
    meta_three.start()

    halves = []

    def pass_on(row, da):
        row[0].wait_recv()
        first = push(da, 3, 0, owner(0, 1))
        to_sibling(da, 3)
        row[1].wait_recv()
        second = push(da, 1, 1, owner(0, 3))
        to_sibling(da, 1)
        halves.append((da, first, second))

    def finish():
        da, first, second = halves.pop(0)
        first.wait_recv()
        second.wait_recv()
        to_sibling(da, 2)

    pass_on(row_own, 0)
    opposite.wait_recv()
    row_far = spread(2) + (push(2, 0, None, owner(0, 2)),)
    to_sibling(2, 0)
    meta_three.wait_recv()
    write_tables(meta_c[0] + meta_c[1], table, keep)
    to_scalar = pltpu.make_async_copy(table, tbl, local_sem.at[3])
    to_scalar.start()
    x_in.wait()
    y_in.wait()
    for i in range(ND):
        block = x_flat[:, i * BLK : (i + 1) * BLK]
        plain[i] = block
        turned[i] = block.T
        plain[AT_Y + i] = y_flat[:, i * BLK : (i + 1) * BLK]
    pass_on(row_left, 3)
    pass_on(row_right, 1)
    finish()
    row_far[0].wait_recv()
    to_sibling(2, 3)
    row_far[1].wait_recv()
    to_sibling(2, 1)
    finish()
    finish()
    row_far[2].wait_recv()
    to_sibling(2, 2)
    to_scalar.wait()
    for copy in to_sib:
        copy.wait_recv()

    def at(row, k):
        return tbl[row, k]

    def weight(i):
        return wgt[pl.ds(i, 2)].reshape(BLK, BLK)

    def dot(left_side, right_side, dims):
        return lax.dot_general(left_side, right_side, (dims, ((), ())), preferred_element_type=jnp.float32)

    def products(rows):
        def step(i, carry):
            for inner in range(4):
                k = 4 * i + inner
                gate = dot(plain[at(ROW_CG, k), rows], weight(at(ROW_SG, k)), ((1,), (0,)))
                up = dot(plain[at(ROW_CU, k), rows], weight(at(ROW_SU, k)), ((1,), (0,)))
                back = dot(plain[at(ROW_CD, k), rows], weight(at(ROW_SD, k)), ((1,), (1,)))
                sigmoid = jax.nn.sigmoid(gate)
                silu = gate * sigmoid
                hid[k, rows] = (silu * up).astype(jnp.bfloat16)
                plain[AT_GATE + k, rows] = (back * up * sigmoid * (1.0 + gate * (1.0 - sigmoid))).astype(
                    jnp.bfloat16
                )
                plain[AT_UP + k, rows] = (back * silu).astype(jnp.bfloat16)
            return carry

        lax.fori_loop(0, TRIPLES // 4, step, 0)

    def widths(rows):
        def step(i, carry):
            made = []
            for inner in range(8):
                m = 8 * i + inner
                made.append(dot(plain[at(ROW_OUT, m), rows], weight(at(ROW_WGT, m)), ((1,), (1,))))
            for inner in range(8):
                m = 8 * i + inner
                sums[m + 1, rows] = made[inner] + sums[m, rows] * keep[m, 0:1, :]
            return carry

        lax.fori_loop(0, ENTRIES // 8, step, 0)

    z_sends = []
    for n in range(ZSENDS):
        here = (pl.ds(n // CUTS * CHUNK, CHUNK), pl.ds(n % CUTS * (D // CUTS), D // CUTS))
        z_sends.append(
            remote(passed.at[here], arriving.at[here], {"segment": lax.rem(z + layers - 1, layers)})
        )

    @pl.when(z > 0)
    def _():
        for n in range(ZSENDS):
            rows = pl.ds(n // CUTS * CHUNK, CHUNK)
            if n % CUTS == 0:
                products(rows)
                widths(rows)
            for i in range(n % CUTS * ND // CUTS, (n % CUTS + 1) * ND // CUTS):
                passed[rows, i * BLK : (i + 1) * BLK] = (
                    plain[AT_Y + i, rows].astype(jnp.float32) + sums[at(ROW_SUM, i), rows]
                ).astype(jnp.bfloat16)
            z_sends[n].start()

    @pl.when(z == 0)
    def _():
        products(pl.ds(0, TOK))

    def turn(i, carry):
        for inner in range(4):
            k = 4 * i + inner
            turned[AT_HID + k] = hid[k].T
        return carry

    lax.fori_loop(0, TRIPLES // 4, turn, 0)

    def term(device, s):
        n = CAP * device + s
        return dot(turned[at(ROW_LEFT, n)], plain[at(ROW_RIGHT, n)], ((1,), (0,)))

    def launch(src, dst, target):
        copy = remote(src, dst, {"fsdp": target})
        copy.start()
        sends.append(copy)
        return copy

    order = (2, 1, 3, 0)
    sib_copies, side_copies = {}, {}

    def fill(da):
        def step(i, carry):
            for inner in range(2):
                db = 2 * i + inner
                for s in range(CAP):
                    sib_out[da, CAP * db + s] = term(sib_owner(da, db), s).astype(jnp.bfloat16)
            return carry

        lax.fori_loop(0, 2, step, 0)
        sib_copies[da] = launch(sib_out.at[da], sib_in.at[da], sibling)

    def pair(da):
        def step(i, carry):
            for inner in range(2):
                db = 2 * i + inner
                for s in range(CAP):
                    n = CAP * db + s
                    value = term(owner(da, db), s) + sib_in[da, n].astype(jnp.float32)
                    pair_out[da, n] = value.astype(jnp.bfloat16)
            return carry

        sib_copies[da].wait_recv()
        lax.fori_loop(0, 2, step, 0)
        side_copies[da] = [
            launch(pair_out.at[da, pl.ds(CAP * db, CAP)], side_in.at[da, pl.ds(CAP * (db - 1), CAP)], owner(0, db))
            for db in (2, 1, 3)
        ]

    fill(2)
    fill(1)
    fill(3)
    pair(2)
    fill(0)
    pair(1)
    pair(3)
    pair(0)

    def ringed(da, s):
        value = pair_out[da, s].astype(jnp.float32)
        for n in range(3):
            value = value + side_in[da, CAP * n + s].astype(jnp.float32)
        return value

    near_copies = []
    for da in order[:3]:
        for copy in side_copies[da]:
            copy.wait_recv()
        for s in range(CAP):
            quad[da - 1, s] = ringed(da, s).astype(jnp.bfloat16)
        near_copies.append(launch(quad.at[da - 1], near_in.at[da - 1], owner(da, 0)))
    for copy in side_copies[0] + near_copies:
        copy.wait_recv()
    for s in range(CAP):
        value = ringed(0, s)
        for n in range(3):
            value = value + near_in[n, s].astype(jnp.float32)
        total[s] = value
    grads_out = pltpu.make_async_copy(total, grads, local_sem.at[5])
    grads_out.start()

    for copy in meta_one + meta_two + [meta_three] + sends:
        copy.wait_send()
    grads_out.wait()

    @pl.when(z == layers - 1)
    def _():
        blank.wait()

    for copy in z_sends:

        @pl.when(z < layers - 1)
        def _(copy=copy):
            copy.wait_recv()

        @pl.when(z > 0)
        def _(copy=copy):
            copy.wait_send()


COPIES = 7 + 3 + 16 + 16 + ZSENDS + 4 + 12 + 3


def body(activations, output_grad, blocks, block_ids, owner_counts):
    bf16, f32 = jnp.bfloat16, jnp.float32
    hbm = pl.BlockSpec(memory_space=pltpu.HBM)
    free = pl.BlockSpec(memory_space=pl.ANY)
    smem = pl.BlockSpec(memory_space=pltpu.SMEM)
    arriving, grads = pl.pallas_call(
        kernel,
        out_shape=(
            jax.ShapeDtypeStruct((TOK, D), bf16),
            jax.ShapeDtypeStruct((CAP, BLK, BLK), f32),
        ),
        in_specs=[smem, smem, hbm, hbm, hbm],
        out_specs=(free, free),
        scratch_shapes=[
            pltpu.VMEM((TOK, D), bf16),
            pltpu.VMEM((TOK, D), bf16),
            pltpu.VMEM((AT_ZERO + 1, TOK, BLK), bf16),
            pltpu.VMEM((AT_NONE + 1, BLK, TOK), bf16),
            pltpu.VMEM((2 * SLOTS + 2, GRAIN, BLK), bf16),
            pltpu.VMEM((4, 8, 128), jnp.int32),
            pltpu.VMEM((4, 8, 128), jnp.int32),
            pltpu.VMEM((2, 8, 128), jnp.int32),
            pltpu.VMEM((16, 128), jnp.int32),
            pltpu.SMEM((16, 128), jnp.int32),
            pltpu.VMEM((ENTRIES, 8, 128), f32),
            pltpu.VMEM((TRIPLES, TOK, BLK), bf16),
            pltpu.VMEM((ENTRIES + 1, TOK, BLK), f32),
            pltpu.VMEM((TOK, D), bf16),
            pltpu.VMEM((TOK, D), bf16),
            pltpu.VMEM((4, 4 * CAP, BLK, BLK), bf16),
            pltpu.VMEM((4, 4 * CAP, BLK, BLK), bf16),
            pltpu.VMEM((4, 4 * CAP, BLK, BLK), bf16),
            pltpu.VMEM((4, 3 * CAP, BLK, BLK), bf16),
            pltpu.VMEM((3, CAP, BLK, BLK), bf16),
            pltpu.VMEM((3, CAP, BLK, BLK), bf16),
            pltpu.VMEM((CAP, BLK, BLK), f32),
            pltpu.SemaphoreType.DMA((6,)),
            pltpu.SemaphoreType.DMA((COPIES,)),
            pltpu.SemaphoreType.DMA((COPIES,)),
        ],
        compiler_params=pltpu.CompilerParams(
            collective_id=0, has_side_effects=True, vmem_limit_bytes=60 * 1024 * 1024
        ),
        name="relay",
    )(
        block_ids,
        owner_counts,
        activations.reshape(TOK, D),
        output_grad.reshape(TOK, D),
        blocks.reshape(PART, GRAIN, BLK),
    )
    return arriving.reshape(1, TOK, D), grads.reshape(1, CAP, BLK, BLK)


def solution(mesh):
    placed = (
        P("segment", "fsdp", None),
        P("segment", "fsdp", None),
        P("segment", "fsdp", None, None),
        P("segment", "fsdp"),
        P("segment", "fsdp"),
    )
    return jax.shard_map(
        body,
        mesh=mesh,
        in_specs=placed,
        out_specs=(P("segment", "fsdp", None), P("segment", "fsdp", None, None)),
        check_vma=False,
    )
```

```python
import jax
import jax.numpy as jnp
from jax import lax
from jax.experimental import pallas as pl
from jax.experimental.pallas import tpu as pltpu
from jax.sharding import PartitionSpec as P

D = 4096
FF = 28672
BLK = 128
CAP = 3
ND = D // BLK
NF = FF // BLK
OWNERS = 32
SLOTS = OWNERS * CAP
PIECE = CAP * BLK
GRAIN = BLK // 2
PART = PIECE // GRAIN
HALF = PART // 2
TOK = 128
TRIPLES = 20
ENTRIES = 2 * TRIPLES
CHUNK = 64
CUTS = 8
ZSENDS = CUTS * (TOK // CHUNK)
MESH = pl.DeviceIdType.MESH

ROW_SG, ROW_SU, ROW_SD, ROW_CG, ROW_CU, ROW_CD = range(6)
ROW_LEFT, ROW_RIGHT, ROW_OUT, ROW_WGT, ROW_SUM = range(6, 11)
AT_Y, AT_GATE, AT_UP, AT_ZERO = ND, 2 * ND, 2 * ND + TRIPLES, 2 * ND + ENTRIES
AT_HID, AT_NONE = ND, ND + TRIPLES


def write_tables(tile, table, keep):
    shape = (128, 128)
    lane = lax.broadcasted_iota(jnp.int32, shape, 1)
    sub = lax.broadcasted_iota(jnp.int32, shape, 0)

    def across(row):
        return jnp.broadcast_to(row, shape)

    def down(row):
        return across(row).T

    def total(mask, values):
        return jnp.sum(jnp.where(mask, values, 0), axis=0, keepdims=True)

    def put(row, values):
        table[row : row + 1, :] = values

    kind, hidden, width, live = (tile[r : r + 1, :] for r in range(4))
    valid = lane[0:1] < SLOTS
    hidden = jnp.where(valid, hidden, 1000)
    thrice = total(down(hidden) < across(hidden), 1)
    key = down(jnp.where(valid, kind * SLOTS + thrice, -1))
    width_down, live_down = down(width), down(live)
    slots, widths, full = [], [], None
    for k in range(3):
        match = (key == k * SLOTS + 3 * lane) & (lane < ND)
        slots.append(down(total(match, sub)))
        widths.append(down(total(match, width_down)))
        alive = total(match, live_down)
        full = alive if full is None else full * alive
    full = down(full)
    place = down(total(sub < lane, full))
    whole = full == 1
    pick = whole & (place == lane)
    for k in range(3):
        put(ROW_SG + k, 2 * (SLOTS + total(pick, slots[k] - SLOTS)))
        put(ROW_CG + k, total(pick, widths[k]) + (AT_Y if k == 2 else 0))
    hit = whole & (3 * sub == across(thrice)) & (sub < ND)
    found, spot = total(hit, 1), total(hit, place)
    left = jnp.where(kind == 2, AT_HID + spot, width)
    right = jnp.where(kind == 2, AT_Y + width, AT_GATE + TRIPLES * kind + spot)
    put(ROW_LEFT, AT_NONE + found * (left - AT_NONE))
    put(ROW_RIGHT, AT_ZERO + found * (right - AT_ZERO))
    late = whole & (place + TRIPLES == lane)
    entry_width = 64 + total(pick, widths[0] - 64) + total(late, widths[1] - 64)
    entry_slot = SLOTS + total(pick, slots[0] - SLOTS) + total(late, slots[1] - SLOTS)
    order = entry_width * 128 + lane[0:1]
    rank = down(total(down(order) < across(order), 1))
    entry_width = down(entry_width)
    chosen = rank == lane
    put(ROW_OUT, AT_GATE + total(chosen, sub))
    put(ROW_WGT, 2 * total(chosen, down(entry_slot)))
    same = total(chosen, entry_width) == total(rank + 1 == lane, entry_width)
    same = down(jnp.where(same & (lane[0:1] > 0), 1, 0)).astype(jnp.float32)
    for m in range(ENTRIES):
        keep[m] = jnp.broadcast_to(same[m : m + 1, :], (8, 128))
    present = total(entry_width == lane, 1) > 0
    put(ROW_SUM, jnp.where(present, total(entry_width <= lane, 1), 0))


def kernel(
    ids,
    count,
    x_hbm,
    y_hbm,
    blocks_hbm,
    arriving,
    grads,
    x_flat,
    y_flat,
    plain,
    turned,
    wgt,
    meta_a,
    meta_b,
    meta_c,
    table,
    tbl,
    keep,
    hid,
    sums,
    passed,
    zeros,
    sib_out,
    sib_in,
    pair_out,
    side_in,
    quad,
    near_in,
    total,
    local_sem,
    send_sem,
    recv_sem,
):
    z, f = lax.axis_index("segment"), lax.axis_index("fsdp")
    layers = lax.axis_size("segment")
    core = lax.rem(f, 2)
    yy, xx = lax.rem(lax.div(f, 2), 4), lax.div(f, 8)
    a = xx * (1 - core) + yy * core
    b = xx * core + yy * (1 - core)

    def owner(da, db):
        return lax.rem(a + da, 4) * (8 - 6 * core) + lax.rem(b + db, 4) * (2 + 6 * core) + core

    def sib_owner(da, db):
        return lax.rem(b + da, 4) * (2 + 6 * core) + lax.rem(a + db, 4) * (8 - 6 * core) + 1 - core

    sibling = f + 1 - 2 * core
    used = [0]

    def remote(src, dst, target):
        i = used[0]
        used[0] = i + 1
        return pltpu.make_async_remote_copy(
            src_ref=src,
            dst_ref=dst,
            send_sem=send_sem.at[i],
            recv_sem=recv_sem.at[i],
            device_id=target,
            device_id_type=MESH,
        )

    own_in = pltpu.make_async_copy(
        blocks_hbm, wgt.at[pl.ds(f * PART, PART)], local_sem.at[0]
    )
    x_in = pltpu.make_async_copy(x_hbm, x_flat, local_sem.at[1])
    y_in = pltpu.make_async_copy(y_hbm, y_flat, local_sem.at[2])
    own_in.start()
    x_in.start()
    y_in.start()

    barrier = pltpu.get_barrier_semaphore()
    partners = [{"fsdp": owner(d, 0)} for d in (1, 2, 3)]
    partners += [{"fsdp": owner(0, d)} for d in (1, 2, 3)]
    partners += [{"fsdp": sibling}]
    partners += [{"segment": lax.rem(z + d, layers)} for d in (1, layers - 1)]
    for partner in partners:
        pl.semaphore_signal(barrier, inc=1, device_id=partner, device_id_type=MESH)

    lane = lax.broadcasted_iota(jnp.int32, (8, 128), 1)
    sub = lax.broadcasted_iota(jnp.int32, (8, 128), 0)
    tile = jnp.zeros((8, 128), jnp.int32)
    alive = jnp.full((8, 128), count[0, 0], jnp.int32)
    for s in range(CAP):
        slot_id = jnp.full((8, 128), ids[0, s], jnp.int32)
        kind = jnp.where(slot_id >= NF * ND, 1, 0) + jnp.where(slot_id >= 2 * NF * ND, 1, 0)
        hidden = (slot_id - kind * (NF * ND)) >> 5
        width = slot_id & (ND - 1)
        live = jnp.where(alive > s, 1, 0)
        column = jnp.where(sub == 0, kind, jnp.where(sub == 1, hidden, jnp.where(sub == 2, width, live)))
        tile = tile + jnp.where((lane == CAP * f + s) & (sub < 4), column, 0)
    meta_a[0] = tile
    wgt[2 * SLOTS :] = jnp.zeros((2, GRAIN, BLK), jnp.bfloat16)
    plain[AT_ZERO] = jnp.zeros((TOK, BLK), jnp.bfloat16)
    turned[AT_NONE] = jnp.zeros((BLK, TOK), jnp.bfloat16)
    sums[0] = jnp.zeros((BLK, BLK), jnp.float32)

    blank = pltpu.make_async_copy(zeros, arriving, local_sem.at[4])

    @pl.when(z == layers - 1)
    def _():
        zeros[...] = jnp.zeros(zeros.shape, jnp.bfloat16)
        blank.start()

    own_in.wait()
    pl.semaphore_wait(barrier, len(partners))

    def piece(da, db, half=None):
        start = owner(da, db) * PART + (HALF if half == 1 else 0)
        return wgt.at[pl.ds(start, PART if half is None else HALF)]

    def forward(da, db, half, target):
        ref = piece(da, db, half)
        copy = remote(ref, ref, {"fsdp": target})
        copy.start()
        return copy

    sends = []

    def to_sibling(da, db):
        copy = forward(da, db, None, sibling)
        to_sib.append(copy)
        sends.append(copy)

    def push(da, db, half, target):
        copy = forward(da, db, half, target)
        sends.append(copy)
        return copy

    def spread(da):
        return push(da, 0, None, owner(0, 1)), push(da, 0, None, owner(0, 3))

    to_sib = []
    meta_one = [remote(meta_a.at[0], meta_a.at[d], {"fsdp": owner(d, 0)}) for d in (1, 2, 3)]
    for copy in meta_one:
        copy.start()
    right, left = push(0, 0, None, owner(1, 0)), push(0, 0, None, owner(3, 0))
    opposite = push(0, 0, None, owner(2, 0))
    row_own = spread(0)
    to_sibling(0, 0)
    for copy in meta_one:
        copy.wait_recv()
    meta_b[0] = meta_a[0] + meta_a[1] + meta_a[2] + meta_a[3]
    meta_two = [remote(meta_b.at[0], meta_b.at[d], {"fsdp": owner(0, d)}) for d in (1, 2, 3)]
    for copy in meta_two:
        copy.start()
    right.wait_recv()
    row_left = spread(3)
    to_sibling(3, 0)
    left.wait_recv()
    row_right = spread(1)
    to_sibling(1, 0)
    for copy in meta_two:
        copy.wait_recv()
    meta_c[0] = meta_b[0] + meta_b[1] + meta_b[2] + meta_b[3]
    meta_three = remote(meta_c.at[0], meta_c.at[1], {"fsdp": sibling})
    meta_three.start()

    halves = []

    def pass_on(row, da):
        row[0].wait_recv()
        first = push(da, 3, 0, owner(0, 1))
        to_sibling(da, 3)
        row[1].wait_recv()
        second = push(da, 1, 1, owner(0, 3))
        to_sibling(da, 1)
        halves.append((da, first, second))

    def finish():
        da, first, second = halves.pop(0)
        first.wait_recv()
        second.wait_recv()
        to_sibling(da, 2)

    pass_on(row_own, 0)
    opposite.wait_recv()
    far = push(2, 0, None, owner(0, 2))
    row_far = spread(2) + (far,)
    to_sibling(2, 0)
    meta_three.wait_recv()
    write_tables(meta_c[0] + meta_c[1], table, keep)
    to_scalar = pltpu.make_async_copy(table, tbl, local_sem.at[3])
    to_scalar.start()
    x_in.wait()
    y_in.wait()
    for i in range(ND):
        block = x_flat[:, i * BLK : (i + 1) * BLK]
        plain[i] = block
        turned[i] = block.T
        plain[AT_Y + i] = y_flat[:, i * BLK : (i + 1) * BLK]
    pass_on(row_left, 3)
    pass_on(row_right, 1)
    finish()
    row_far[0].wait_recv()
    to_sibling(2, 3)
    row_far[1].wait_recv()
    to_sibling(2, 1)
    finish()
    finish()
    row_far[2].wait_recv()
    to_sibling(2, 2)
    to_scalar.wait()
    for copy in to_sib:
        copy.wait_recv()

    def at(row, k):
        return tbl[row, k]

    def weight(i):
        return wgt[pl.ds(i, 2)].reshape(BLK, BLK)

    def dot(left_side, right_side, dims):
        return lax.dot_general(left_side, right_side, (dims, ((), ())), preferred_element_type=jnp.float32)

    def products(rows):
        def step(i, carry):
            for inner in range(4):
                k = 4 * i + inner
                gate = dot(plain[at(ROW_CG, k), rows], weight(at(ROW_SG, k)), ((1,), (0,)))
                up = dot(plain[at(ROW_CU, k), rows], weight(at(ROW_SU, k)), ((1,), (0,)))
                back = dot(plain[at(ROW_CD, k), rows], weight(at(ROW_SD, k)), ((1,), (1,)))
                sigmoid = jax.nn.sigmoid(gate)
                silu = gate * sigmoid
                hid[k, rows] = (silu * up).astype(jnp.bfloat16)
                plain[AT_GATE + k, rows] = (back * up * sigmoid * (1.0 + gate * (1.0 - sigmoid))).astype(
                    jnp.bfloat16
                )
                plain[AT_UP + k, rows] = (back * silu).astype(jnp.bfloat16)
            return carry

        lax.fori_loop(0, TRIPLES // 4, step, 0)

    def widths(rows):
        def step(i, carry):
            made = []
            for inner in range(20):
                m = 20 * i + inner
                made.append(dot(plain[at(ROW_OUT, m), rows], weight(at(ROW_WGT, m)), ((1,), (1,))))
            for inner in range(20):
                m = 20 * i + inner
                sums[m + 1, rows] = made[inner] + sums[m, rows] * keep[m, 0:1, :]
            return carry

        lax.fori_loop(0, ENTRIES // 20, step, 0)

    z_sends = []
    for n in range(ZSENDS):
        here = (pl.ds(n // CUTS * CHUNK, CHUNK), pl.ds(n % CUTS * (D // CUTS), D // CUTS))
        z_sends.append(
            remote(passed.at[here], arriving.at[here], {"segment": lax.rem(z + layers - 1, layers)})
        )

    @pl.when(z > 0)
    def _():
        for n in range(ZSENDS):
            rows = pl.ds(n // CUTS * CHUNK, CHUNK)
            if n % CUTS == 0:
                products(rows)
                widths(rows)
            for i in range(n % CUTS * ND // CUTS, (n % CUTS + 1) * ND // CUTS):
                passed[rows, i * BLK : (i + 1) * BLK] = (
                    plain[AT_Y + i, rows].astype(jnp.float32) + sums[at(ROW_SUM, i), rows]
                ).astype(jnp.bfloat16)
            z_sends[n].start()

    @pl.when(z == 0)
    def _():
        products(pl.ds(0, TOK))

    def turn(i, carry):
        for inner in range(4):
            k = 4 * i + inner
            turned[AT_HID + k] = hid[k].T
        return carry

    lax.fori_loop(0, TRIPLES // 4, turn, 0)

    def term(device, s):
        n = CAP * device + s
        return dot(turned[at(ROW_LEFT, n)], plain[at(ROW_RIGHT, n)], ((1,), (0,)))

    def launch(src, dst, target):
        copy = remote(src, dst, {"fsdp": target})
        copy.start()
        sends.append(copy)
        return copy

    order = (2, 1, 3, 0)
    sib_copies, side_copies = {}, {}

    def fill(da):
        def step(i, carry):
            for inner in range(2):
                db = 2 * i + inner
                for s in range(CAP):
                    sib_out[da, CAP * db + s] = term(sib_owner(da, db), s).astype(jnp.bfloat16)
            return carry

        lax.fori_loop(0, 2, step, 0)
        sib_copies[da] = launch(sib_out.at[da], sib_in.at[da], sibling)

    def pair(da):
        def step(i, carry):
            for inner in range(2):
                db = 2 * i + inner
                for s in range(CAP):
                    n = CAP * db + s
                    value = term(owner(da, db), s) + sib_in[da, n].astype(jnp.float32)
                    pair_out[da, n] = value.astype(jnp.bfloat16)
            return carry

        sib_copies[da].wait_recv()
        lax.fori_loop(0, 2, step, 0)
        side_copies[da] = [
            launch(pair_out.at[da, pl.ds(CAP * db, CAP)], side_in.at[da, pl.ds(CAP * (db - 1), CAP)], owner(0, db))
            for db in (2, 1, 3)
        ]

    fill(2)
    fill(1)
    fill(3)
    pair(2)
    fill(0)
    pair(1)
    pair(3)
    pair(0)

    def ringed(da, s):
        value = pair_out[da, s].astype(jnp.float32)
        for n in range(3):
            value = value + side_in[da, CAP * n + s].astype(jnp.float32)
        return value

    near_copies = []
    for da in order[:3]:
        for copy in side_copies[da]:
            copy.wait_recv()
        for s in range(CAP):
            quad[da - 1, s] = ringed(da, s).astype(jnp.bfloat16)
        near_copies.append(launch(quad.at[da - 1], near_in.at[da - 1], owner(da, 0)))
    for copy in side_copies[0] + near_copies:
        copy.wait_recv()
    for s in range(CAP):
        value = ringed(0, s)
        for n in range(3):
            value = value + near_in[n, s].astype(jnp.float32)
        total[s] = value
    grads_out = pltpu.make_async_copy(total, grads, local_sem.at[5])
    grads_out.start()

    for copy in meta_one + meta_two + [meta_three] + sends:
        copy.wait_send()
    grads_out.wait()

    @pl.when(z == layers - 1)
    def _():
        blank.wait()

    for copy in z_sends:

        @pl.when(z < layers - 1)
        def _(copy=copy):
            copy.wait_recv()

        @pl.when(z > 0)
        def _(copy=copy):
            copy.wait_send()


COPIES = 7 + 3 + 16 + 16 + ZSENDS + 4 + 12 + 3


def body(activations, output_grad, blocks, block_ids, owner_counts):
    bf16, f32 = jnp.bfloat16, jnp.float32
    hbm = pl.BlockSpec(memory_space=pltpu.HBM)
    free = pl.BlockSpec(memory_space=pl.ANY)
    smem = pl.BlockSpec(memory_space=pltpu.SMEM)
    arriving, grads = pl.pallas_call(
        kernel,
        out_shape=(
            jax.ShapeDtypeStruct((TOK, D), bf16),
            jax.ShapeDtypeStruct((CAP, BLK, BLK), f32),
        ),
        in_specs=[smem, smem, hbm, hbm, hbm],
        out_specs=(free, free),
        scratch_shapes=[
            pltpu.VMEM((TOK, D), bf16),
            pltpu.VMEM((TOK, D), bf16),
            pltpu.VMEM((AT_ZERO + 1, TOK, BLK), bf16),
            pltpu.VMEM((AT_NONE + 1, BLK, TOK), bf16),
            pltpu.VMEM((2 * SLOTS + 2, GRAIN, BLK), bf16),
            pltpu.VMEM((4, 8, 128), jnp.int32),
            pltpu.VMEM((4, 8, 128), jnp.int32),
            pltpu.VMEM((2, 8, 128), jnp.int32),
            pltpu.VMEM((16, 128), jnp.int32),
            pltpu.SMEM((16, 128), jnp.int32),
            pltpu.VMEM((ENTRIES, 8, 128), f32),
            pltpu.VMEM((TRIPLES, TOK, BLK), bf16),
            pltpu.VMEM((ENTRIES + 1, TOK, BLK), f32),
            pltpu.VMEM((TOK, D), bf16),
            pltpu.VMEM((TOK, D), bf16),
            pltpu.VMEM((4, 4 * CAP, BLK, BLK), bf16),
            pltpu.VMEM((4, 4 * CAP, BLK, BLK), bf16),
            pltpu.VMEM((4, 4 * CAP, BLK, BLK), bf16),
            pltpu.VMEM((4, 3 * CAP, BLK, BLK), bf16),
            pltpu.VMEM((3, CAP, BLK, BLK), bf16),
            pltpu.VMEM((3, CAP, BLK, BLK), bf16),
            pltpu.VMEM((CAP, BLK, BLK), f32),
            pltpu.SemaphoreType.DMA((6,)),
            pltpu.SemaphoreType.DMA((COPIES,)),
            pltpu.SemaphoreType.DMA((COPIES,)),
        ],
        compiler_params=pltpu.CompilerParams(
            collective_id=0, has_side_effects=True, vmem_limit_bytes=60 * 1024 * 1024
        ),
        name="relay",
    )(
        block_ids,
        owner_counts,
        activations.reshape(TOK, D),
        output_grad.reshape(TOK, D),
        blocks.reshape(PART, GRAIN, BLK),
    )
    return arriving.reshape(1, TOK, D), grads.reshape(1, CAP, BLK, BLK)


def solution(mesh):
    placed = (
        P("segment", "fsdp", None),
        P("segment", "fsdp", None),
        P("segment", "fsdp", None, None),
        P("segment", "fsdp"),
        P("segment", "fsdp"),
    )
    return jax.shard_map(
        body,
        mesh=mesh,
        in_specs=placed,
        out_specs=(P("segment", "fsdp", None), P("segment", "fsdp", None, None)),
        check_vma=False,
    )
```
